32 devices in a mesh: groups: 2 (over y), pool: 4 (over z), sub: 2 (over x), chip: 2 (over core).
Axes of the slice: x: 2, y: 2, z: 4, core: 2. Of those that a mesh axis runs over, the one named last changes fastest.
Arguments:
- hidden: bfloat16 [1024, 4096], P(('groups', 'pool', 'sub', 'chip')), parts along dimension 0, may hold values from -6 to 6
- query_weight_matrix: bfloat16 [4096, 4096], P(None, 'pool'), may hold values from -0.09375 to 0.09375
- adapter_down_weight: bfloat16 [64, 64, 4096], P('pool', None, ('sub', 'chip')), may hold values from -0.09375 to 0.09375
- adapter_up_weight: bfloat16 [64, 64, 4096], P('pool', None, ('sub', 'chip')), may hold values from -0.75 to 0.75
- adapter_index_rows: int32 [1024], P(('groups', 'pool', 'sub', 'chip')), parts along dimension 0, may hold values from 0 to 63, as said below
Outputs:
- query: bfloat16 [1024, 4096], P(('groups', 'pool', 'sub', 'chip')), parts along dimension 0
The draws below stay inside these ranges and needn't reach their ends.
There are 2 independent parts, one for each index of `groups`. The reference program is written for one: setup_inputs(seed, part) draws one part's arguments, and reference() takes and returns one part's arrays. A program takes and returns all parts, laid end to end along the dimension named above; an argument that names none is the same for every part. Nothing has to cross between parts.
Inputs may be any that keep to these rules, and one draw needn't show every extreme that they name: A row's owner is adapter_index_rows // 16. In each aligned block of 32 rows (the rows of one device) at most 12 rows have one owner, and in every block some owner has exactly 12 rows.
All inputs are finite; a program needn't handle non-finite values.
Results may differ from the reference program's by a relative error of at most 0.0052.
Values may be sent and summed in bfloat16 or wider, within the bound.
A program may use at most 64 MiB of HBM per device.

```python
import jax
import jax.numpy as jnp
from jax import lax

MODEL_WIDTH = 4096
ADAPTER_RANK = 64
ADAPT_POOL = 16
ROW_DEV = 32
OWNERS = 4
SHARDS = 4
ADAPTER_TOTAL = 64
CAP = 12
ROWS = 512


def draw_adapter_index_rows(key, part):
    blocks = ROWS // ROW_DEV
    full_count = ROW_DEV // CAP
    leftover = ROW_DEV - full_count * CAP
    group_base = jax.random.fold_in(key, 9001)

    def one_block(index):
        group_key = jax.random.fold_in(group_base, index // SHARDS)
        order = jax.random.permutation(group_key, OWNERS).astype(jnp.int32)
        full_owners = order[:full_count]
        block_key = jax.random.fold_in(key, index + 11)
        others = jax.random.permutation(jax.random.fold_in(block_key, 1), order[full_count:])
        owners = jnp.concatenate([jnp.repeat(full_owners, CAP), jnp.tile(others, CAP)[:leftover]])
        owners = jax.random.permutation(jax.random.fold_in(block_key, 2), owners)
        within = jax.random.randint(jax.random.fold_in(block_key, 3), (ROW_DEV,), 0, ADAPT_POOL)
        return owners * ADAPT_POOL + within
    return jax.vmap(one_block)(jnp.arange(blocks, dtype=jnp.int32)).reshape(ROWS).astype(jnp.int32)


def block_scale(stream_key, dims, shards, low, top_value):
    def one(position, parts):
        draws = jax.random.uniform(jax.random.fold_in(jax.random.fold_in(stream_key, 6), position), (parts,), jnp.float32, low / len(shards), top_value / len(shards))
        return jnp.repeat(jnp.exp(draws), dims[position] // parts).reshape((-1,) + (1,) * (len(dims) - position - 1))

    level = one(*shards[0])
    for cut in shards[1:]:
        level = level * one(*cut)
    return level


def centred(own_key, shape, spread, most, shards=(), kind=jnp.bfloat16):
    loudness = block_scale(own_key, shape, shards, -0.22, 0.18) if shards else 1.0
    values = jax.random.normal(own_key, shape, jnp.float32) * spread * loudness
    return jnp.minimum(jnp.maximum(values, -most), most).astype(kind)


def setup_inputs(seed: int = 0, part: int = 0) -> dict:
    key_list = jax.random.split(jax.random.key(seed), 6)
    part_splits = jax.random.split(jax.random.fold_in(key_list[5], part), 6)
    return {
        "hidden": centred(part_splits[0], (ROWS, MODEL_WIDTH), 1.0, 6.0, ((0, 16),)),
        "query_weight_matrix": centred(key_list[1], (MODEL_WIDTH, MODEL_WIDTH), MODEL_WIDTH ** -0.5, 0.09375, ((1, 4),)),
        "adapter_down_weight": centred(key_list[2], (ADAPTER_TOTAL, ADAPTER_RANK, MODEL_WIDTH), MODEL_WIDTH ** -0.5, 0.09375, ((0, 4), (2, 4))),
        "adapter_up_weight": centred(key_list[3], (ADAPTER_TOTAL, ADAPTER_RANK, MODEL_WIDTH), ADAPTER_RANK ** -0.5, 0.75, ((0, 4), (2, 4))),
        "adapter_index_rows": draw_adapter_index_rows(jax.random.fold_in(jax.random.fold_in(key_list[5], part), 71), part),
    }


ADAPTER_SCALE = 0.5


def reference(hidden, query_weight_matrix, adapter_down_weight, adapter_up_weight, adapter_index_rows):
    base = jnp.dot(hidden, query_weight_matrix, preferred_element_type=jnp.float32).astype(jnp.bfloat16)
    blocks = hidden.shape[0] // ROW_DEV
    block_rows = hidden.reshape(blocks, ROW_DEV, MODEL_WIDTH)
    block_adapters = adapter_index_rows.reshape(blocks, ROW_DEV)

    def one_block(pair):
        rows_here, resident_adapters = pair
        down_matrix = adapter_down_weight[resident_adapters].astype(jnp.float32)
        projected_down = jnp.einsum("rd,rkd->rk", rows_here.astype(jnp.float32), down_matrix).astype(jnp.bfloat16)
        projected_down = lax.optimization_barrier(projected_down).astype(jnp.float32)
        projected_up = adapter_up_weight[resident_adapters].astype(jnp.float32)
        return (ADAPTER_SCALE * jnp.einsum("fj,fjs->fs", projected_down, projected_up)).astype(jnp.bfloat16)

    update_term = lax.map(one_block, (block_rows, block_adapters)).reshape(hidden.shape[0], MODEL_WIDTH)
    base_wide = lax.optimization_barrier(base).astype(jnp.float32)
    delta_wide = lax.optimization_barrier(update_term).astype(jnp.float32)
    return (base_wide + delta_wide).astype(jnp.bfloat16)
```

```python
import functools

import jax
import jax.numpy as jnp
from jax import lax
from jax.experimental import pallas as pl
from jax.experimental.pallas import tpu as pltpu
from jax.sharding import PartitionSpec as P

ADAPTER_SCALE = 0.5
SLOTS = 16
HELD = 12
META = 128
MESH = pl.DeviceIdType.MESH
F32 = jnp.float32
BF16 = jnp.bfloat16


def tile_of(extent):
    return 256 if extent % 256 == 0 else extent


def kernel(
    pools, chips, shards, stack,
    h_hbm, idx_hbm, w_hbm, dn_hbm, up_hbm, out_ref,
    x, w, dn, up, picked, rows, low_out, low, delta, home_delta, base, home_base, acc,
    idx_ref, wsem, hright, hleft, hrecv, rsend, rrecv, lsend, lrecv, bsend, brecv, dsend, drecv,
):
    p = lax.axis_index("pool")
    me = lax.axis_index("sub") * chips + lax.axis_index("chip")
    rows_dev, width = h_hbm.shape
    cols = w.shape[1]
    part = width // shards
    half = width // 2
    quarter = part // 4
    ranks = dn.shape[0] // stack
    tiles = stack * ranks // 256
    each = 256 // ranks
    many = shards * SLOTS

    def where_is(z, sh):
        return {"pool": z, "sub": sh // chips, "chip": sh % chips}

    def rcopy(src, dst, ssem, rsem, z, sh):
        return pltpu.make_async_remote_copy(
            src_ref=src, dst_ref=dst, send_sem=ssem, recv_sem=rsem,
            device_id=where_is(z, sh), device_id_type=MESH,
        )

    peers = [(me + d) % shards for d in range(1, shards)]

    barrier = pltpu.get_barrier_semaphore()

    def greet(z, sh):
        pl.semaphore_signal(barrier, inc=1, device_id=where_is(z, sh), device_id_type=MESH)

    @pl.when(p >= 1)
    def _():
        greet(p - 1, me)

    @pl.when(p + 1 < pools)
    def _():
        greet(p + 1, me)

    for sh in peers:
        greet(p, sh)

    loads = [
        pltpu.make_async_copy(w_hbm.at[pl.ds(0, half)], w.at[pl.ds(0, half)], wsem.at[0]),
        pltpu.make_async_copy(w_hbm.at[pl.ds(half, half)], w.at[pl.ds(half, half)], wsem.at[1]),
        pltpu.make_async_copy(dn_hbm, dn, wsem.at[2]),
        pltpu.make_async_copy(up_hbm, up, wsem.at[3]),
        pltpu.make_async_copy(h_hbm, x.at[p, :, pl.ds(META, width)], wsem.at[4]),
    ]
    ic = pltpu.make_async_copy(idx_hbm, idx_ref, wsem.at[5])
    ic.start()
    for i in (4, 0, 2, 1, 3):
        loads[i].start()
    ic.wait()

    square = (rows_dev, rows_dev)
    down_axis = lax.broadcasted_iota(jnp.int32, square, 0)
    along = lax.broadcasted_iota(jnp.int32, square, 1)
    index = jnp.broadcast_to(idx_ref[...], square).astype(F32)
    column = jnp.sum(jnp.where(down_axis == along, index, 0.0), axis=1, keepdims=True)
    column = column.astype(jnp.int32)
    owner_column = column // stack
    first = lax.broadcasted_iota(jnp.int32, (rows_dev, META), 1) == 0
    meta = jnp.where(first, owner_column, column - owner_column * stack)
    x[p, :, pl.ds(0, META)] = meta.astype(F32).astype(BF16)

    greeters = jnp.minimum(p, 1) + jnp.minimum(pools - 1 - p, 1) + shards - 1
    pl.semaphore_wait(barrier, greeters)
    loads[4].wait()

    def piece(q):
        return pl.ds(META + q * part, part)

    def sent(q):
        return pl.ds(0, META + part) if q == 0 else piece(q)

    def to_right(b, q):
        ref = x.at[b, :, sent(q)]
        return rcopy(ref, ref, hright.at[b, q], hrecv.at[b, q], p + 1, me)

    def to_left(b, q):
        ref = x.at[b, :, sent(q)]
        return rcopy(ref, ref, hleft.at[b, q], hrecv.at[b, q], p - 1, me)

    for q in range(shards):
        @pl.when(p + 1 < pools)
        def _():
            to_right(p, q).start()

        @pl.when(p >= 1)
        def _():
            to_left(p, q).start()

    before = jnp.where(down_axis < along, 1.0, 0.0).astype(BF16)

    def selection(b):
        pick_owner = lax.broadcasted_iota(jnp.int32, (SLOTS, META), 1) == 0
        owner = lax.dot_general(
            jnp.where(pick_owner, 1.0, 0.0).astype(BF16), x[b, :, pl.ds(0, META)],
            (((1,), (1,)), ((), ())), preferred_element_type=F32,
        )
        owned = jnp.where(owner == p.astype(F32), 1.0, 0.0)
        rank = jnp.dot(owned.astype(BF16), before, preferred_element_type=F32)
        slot = lax.broadcasted_iota(jnp.int32, (SLOTS, rows_dev), 0).astype(F32)
        return jnp.where(rank == slot, owned, 0.0).astype(BF16)

    def pick(b, chosen, tag, q):
        got = jnp.dot(chosen, x[b, :, piece(q)], preferred_element_type=F32).astype(BF16)

        @pl.when(q != me)
        def _():
            picked[b, q, :, pl.ds(0, META)] = tag
            picked[b, q, :, pl.ds(META, part)] = got
            rcopy(picked.at[b, q], rows.at[b, me], rsend.at[b, q], rrecv.at[b, me], p, q).start()

        @pl.when(q == me)
        def _():
            rows[b, me, :, pl.ds(0, META)] = tag
            rows[b, me, :, pl.ds(META, part)] = got

    def select_tag(b):
        chosen = selection(b)
        tag = jnp.dot(chosen, x[b, :, pl.ds(0, META)], preferred_element_type=F32).astype(BF16)
        return chosen, tag

    def arrive(b, q, from_left):
        rcopy(
            x.at[b, :, sent(q)], x.at[b, :, sent(q)], hright.at[b, q], hrecv.at[b, q], p, peers[0]
        ).wait_recv()
        if from_left:
            @pl.when(p + 1 < pools)
            def _():
                to_right(b, q).start()
        else:
            @pl.when(p >= 1)
            def _():
                to_left(b, q).start()

    def receive(b, from_left):
        arrive(b, 0, from_left)
        chosen, tag = select_tag(b)
        pick(b, chosen, tag, 0)
        for q in range(1, shards):
            arrive(b, q, from_left)
            pick(b, chosen, tag, q)

    def project(b, k, last):
        tile = tile_of(cols)

        for j in range(cols // tile):
            at = pl.ds(j * tile, tile)
            term = jnp.dot(
                x[b, :, pl.ds(META + k * half, half)], w[pl.ds(k * half, half), at],
                preferred_element_type=F32,
            )
            if last:
                base[b, :, at] = (acc[b, :, at] + term).astype(BF16)
            else:
                acc[b, :, at] = term

    mine_cols = pl.ds(pl.multiple_of(p * cols, 128), cols)
    mine_slots = pl.ds(pl.multiple_of(p * SLOTS, SLOTS), SLOTS)

    def base_copy(b):
        return rcopy(base.at[b], home_base.at[:, mine_cols], bsend.at[b], brecv.at[p], b, me)

    def delta_copy(b, sh):
        return rcopy(
            delta.at[b, sh], home_delta.at[me, mine_slots], dsend.at[b, sh], drecv.at[p, me], b, sh
        )

    lane = lax.broadcasted_iota(jnp.int32, (many, 256), 1) // ranks
    lower = lax.broadcasted_iota(jnp.int32, (many // 2, 128), 1) < 64

    def adapter_of(b):
        tag = rows[b, :, :, pl.ds(0, META)].reshape(many, META).astype(F32)
        return tag[:, 1:2].astype(jnp.int32)

    def shrink(b):
        for sh in peers:
            rcopy(rows.at[b, sh], rows.at[b, sh], rsend.at[b, sh], rrecv.at[b, sh], p, sh).wait_recv()
        adapter = adapter_of(b)
        here = rows[b, :, :, pl.ds(META, part)].reshape(many, part)
        total = jnp.zeros((many, 128), F32)
        for j in range(tiles):
            term = lax.dot_general(
                here, dn[pl.ds(j * 256, 256), :], (((1,), (1,)), ((), ())),
                preferred_element_type=F32,
            )
            term = jnp.where(lane + j * each == adapter, term, 0.0)
            total = total + term[:, :128] + term[:, 128:]
        total = total + pltpu.roll(total, 64, 1)
        packed = jnp.where(lower, total[: many // 2], total[many // 2 :])
        low_out[b] = packed
        low[b, me] = packed
        for sh in peers:
            rcopy(low_out.at[b], low.at[b, me], lsend.at[b, sh], lrecv.at[b, me], p, sh).start()

    def grow(b):
        for sh in peers:
            rcopy(low_out.at[b], low.at[b, sh], lsend.at[b, sh], lrecv.at[b, sh], p, sh).wait_recv()
        adapter = adapter_of(b)
        both = low[b, 0]
        for sh in range(1, shards):
            both = both + low[b, sh]
        both = both.astype(BF16).astype(F32)
        turned = pltpu.roll(both, 64, 1)
        full = jnp.concatenate(
            [jnp.where(lower, both, turned), jnp.where(lower, turned, both)], axis=0
        )
        full = jnp.concatenate([full, full], axis=1)
        spread = jnp.concatenate(
            [
                jnp.where(lane + j * each == adapter, full, 0.0).astype(BF16)
                for j in range(tiles)
            ],
            axis=1,
        )
        rest = jnp.dot(spread, up[:, pl.ds(3 * quarter, quarter)], preferred_element_type=F32)
        top = lax.broadcasted_iota(jnp.int32, (many, quarter), 0) % SLOTS < HELD
        for j in range(3):
            at = pl.ds(j * quarter, quarter)
            term = jnp.dot(spread, up[:, at], preferred_element_type=F32)
            term = jnp.where(top, term, pltpu.roll(rest, HELD - 4 * j, 0))
            delta[b, :, :, at] = (ADAPTER_SCALE * term).astype(BF16).reshape(shards, SLOTS, quarter)
        for sh in range(shards):
            @pl.when(jnp.logical_or(b != p, sh != me))
            def _():
                delta_copy(b, sh).start()

            @pl.when(jnp.logical_and(b == p, sh == me))
            def _():
                home_delta[me, mine_slots] = delta[b, sh]

    def both_sides(t, f):
        def turn(i, c):
            b = jnp.where(i == 0, p - t, p + t)
            valid = jnp.logical_and(jnp.logical_and(b >= 0, b < pools), jnp.logical_or(i == 0, t > 0))

            @pl.when(valid)
            def _():
                f(b)
            return c

        lax.fori_loop(0, 2, turn, 0)

    chosen, tag = select_tag(p)
    for q in range(shards):
        pick(p, chosen, tag, q)

    def step(t, carry):
        @pl.when(t == 0)
        def _():
            loads[0].wait()
        both_sides(t, lambda b: project(b, 0, False))

        @pl.when(t == 0)
        def _():
            loads[2].wait()
        both_sides(t, shrink)

        @pl.when(t == 0)
        def _():
            loads[1].wait()

        def finish(b):
            project(b, 1, True)

            @pl.when(b != p)
            def _():
                base_copy(b).start()

            @pl.when(b == p)
            def _():
                home_base[:, mine_cols] = base[b]

        inner = jnp.logical_and(jnp.logical_and(p - t >= 0, p + t < pools), t > 0)

        def phase(i, c):
            @pl.when(i == jnp.where(inner, 1, 0))
            def _():
                both_sides(t, finish)

            @pl.when(i == jnp.where(inner, 0, 1))
            def _():
                @pl.when(p - 1 - t >= 0)
                def _():
                    receive(p - 1 - t, True)

                @pl.when(p + 1 + t < pools)
                def _():
                    receive(p + 1 + t, False)
            return c

        lax.fori_loop(0, 2, phase, 0)

        @pl.when(t == 0)
        def _():
            loads[3].wait()
        both_sides(t, grow)
        return carry

    lax.fori_loop(0, pools, step, 0)

    slots = pools * SLOTS
    lanes = lax.broadcasted_iota(jnp.int32, (rows_dev, slots), 1)
    owner = jnp.where(owner_column == lanes // SLOTS, 1.0, 0.0)
    after = jnp.where(down_axis > along, 1.0, 0.0).astype(BF16)
    rank = jnp.dot(after, owner.astype(BF16), preferred_element_type=F32)
    seat = lanes % SLOTS
    place = jnp.where(rank == seat.astype(F32), owner, 0.0).astype(BF16)
    tails = [
        jnp.where(
            jnp.logical_and(seat >= HELD, rank == (seat - HELD + 4 * k).astype(F32)), owner, 0.0
        ).astype(BF16)
        for k in range(3)
    ]

    places = jnp.concatenate([place] + tails, axis=0)

    def base_wait(z, carry):
        @pl.when(z != p)
        def _():
            dst = home_base.at[:, pl.ds(pl.multiple_of(z * cols, 128), cols)]
            rcopy(base.at[z], dst, bsend.at[z], brecv.at[z], z, me).wait_recv()
        return carry

    lax.fori_loop(0, pools, base_wait, 0)

    for sh in range(shards):
        def delta_wait(z, carry):
            @pl.when(jnp.logical_or(z != p, sh != me))
            def _():
                dst = home_delta.at[sh, pl.ds(pl.multiple_of(z * SLOTS, SLOTS), SLOTS)]
                rcopy(delta.at[z, sh], dst, dsend.at[z, sh], drecv.at[z, sh], z, sh).wait_recv()
            return carry

        lax.fori_loop(0, pools, delta_wait, 0)
        start = sh * part
        wide = 3 * quarter
        term = jnp.dot(places, home_delta[sh], preferred_element_type=F32)
        at = pl.ds(start, wide)
        out_ref[:, at] = (home_base[:, at].astype(F32) + term[:rows_dev]).astype(BF16)
        rest = term[rows_dev : 2 * rows_dev, :quarter]
        rest = rest + term[2 * rows_dev : 3 * rows_dev, quarter : 2 * quarter]
        rest = rest + term[3 * rows_dev :, 2 * quarter :]
        at = pl.ds(start + wide, quarter)
        out_ref[:, at] = (home_base[:, at].astype(F32) + rest).astype(BF16)

    def drain(b, carry):
        for q in range(shards):
            @pl.when(jnp.logical_and(b <= p, p + 1 < pools))
            def _():
                to_right(b, q).wait_send()

            @pl.when(jnp.logical_and(b >= p, p >= 1))
            def _():
                to_left(b, q).wait_send()

            @pl.when(q != me)
            def _():
                rcopy(picked.at[b, q], rows.at[b, me], rsend.at[b, q], rrecv.at[b, me], p, q).wait_send()
                rcopy(low_out.at[b], low.at[b, me], lsend.at[b, q], lrecv.at[b, me], p, q).wait_send()

            @pl.when(jnp.logical_or(b != p, q != me))
            def _():
                delta_copy(b, q).wait_send()

        @pl.when(b != p)
        def _():
            base_copy(b).wait_send()
        return carry

    lax.fori_loop(0, pools, drain, 0)


def local(hidden, query_weight_matrix, adapter_down_weight, adapter_up_weight, adapter_index_rows):
    pools = lax.axis_size("pool")
    chips = lax.axis_size("chip")
    shards = lax.axis_size("sub") * chips
    row_count, width = hidden.shape
    cols = query_weight_matrix.shape[1]
    stack, ranks, part = adapter_down_weight.shape
    if 2 + row_count // (pools - 1) > HELD:
        raise ValueError("owner overflow")
    dma = pltpu.SemaphoreType.DMA
    vmem = pl.BlockSpec(memory_space=pltpu.VMEM)
    hbm = pl.BlockSpec(memory_space=pl.ANY)
    return pl.pallas_call(
        functools.partial(kernel, pools, chips, shards, stack),
        out_shape=jax.ShapeDtypeStruct((row_count, width), BF16),
        in_specs=[hbm, hbm, hbm, hbm, hbm],
        out_specs=vmem,
        scratch_shapes=[
            pltpu.VMEM((pools, row_count, META + width), BF16),
            pltpu.VMEM((width, cols), BF16),
            pltpu.VMEM((stack * ranks, part), BF16),
            pltpu.VMEM((stack * ranks, part), BF16),
            pltpu.VMEM((pools, shards, SLOTS, META + part), BF16),
            pltpu.VMEM((pools, shards, SLOTS, META + part), BF16),
            pltpu.VMEM((pools, shards * SLOTS // 2, 128), F32),
            pltpu.VMEM((pools, shards, shards * SLOTS // 2, 128), F32),
            pltpu.VMEM((pools, shards, SLOTS, part - part // 4), BF16),
            pltpu.VMEM((shards, pools * SLOTS, part - part // 4), BF16),
            pltpu.VMEM((pools, row_count, cols), BF16),
            pltpu.VMEM((row_count, width), BF16),
            pltpu.VMEM((pools, row_count, cols), F32),
            pltpu.VMEM((1, row_count), jnp.int32),
            dma((6,)),
            dma((pools, shards)),
            dma((pools, shards)),
            dma((pools, shards)),
            dma((pools, shards)),
            dma((pools, shards)),
            dma((pools, shards)),
            dma((pools, shards)),
            dma((pools,)),
            dma((pools,)),
            dma((pools, shards)),
            dma((pools, shards)),
        ],
        compiler_params=pltpu.CompilerParams(
            collective_id=0, has_side_effects=True, vmem_limit_bytes=3428 * 16384
        ),
    )(
        hidden,
        adapter_index_rows[None, :],
        query_weight_matrix,
        adapter_down_weight.reshape(stack * ranks, part),
        adapter_up_weight.reshape(stack * ranks, part),
    )


def solution(mesh):
    in_specs = (
        P(("groups", "pool", "sub", "chip"), None),
        P(None, "pool"),
        P("pool", None, ("sub", "chip")),
        P("pool", None, ("sub", "chip")),
        P(("groups", "pool", "sub", "chip")),
    )
    out_specs = P(("groups", "pool", "sub", "chip"), None)
    return jax.shard_map(local, mesh=mesh, in_specs=in_specs, out_specs=out_specs, check_vma=False)
```

```python
import functools

import jax
import jax.numpy as jnp
from jax import lax
from jax.experimental import pallas as pl
from jax.experimental.pallas import tpu as pltpu
from jax.sharding import PartitionSpec as P

ADAPTER_SCALE = 0.5
SLOTS = 16
HELD = 12
META = 128
MESH = pl.DeviceIdType.MESH
F32 = jnp.float32
BF16 = jnp.bfloat16


def tile_of(extent):
    return 256 if extent % 256 == 0 else extent


def kernel(
    pools, chips, shards, stack,
    h_hbm, idx_hbm, w_hbm, dn_hbm, up_hbm, out_ref,
    x, w, dn, up, picked, rows, low_out, low, delta, home_delta, base, home_base, acc,
    idx_ref, wsem, hright, hleft, hrecv, rsend, rrecv, lsend, lrecv, bsend, brecv, dsend, drecv,
):
    p = lax.axis_index("pool")
    me = lax.axis_index("sub") * chips + lax.axis_index("chip")
    rows_dev, width = h_hbm.shape
    cols = w.shape[1]
    part = width // shards
    half = width // 2
    quarter = part // 4
    ranks = dn.shape[0] // stack
    tiles = stack * ranks // 256
    each = 256 // ranks
    many = shards * SLOTS

    def where_is(z, sh):
        return {"pool": z, "sub": sh // chips, "chip": sh % chips}

    def rcopy(src, dst, ssem, rsem, z, sh):
        return pltpu.make_async_remote_copy(
            src_ref=src, dst_ref=dst, send_sem=ssem, recv_sem=rsem,
            device_id=where_is(z, sh), device_id_type=MESH,
        )

    peers = [(me + d) % shards for d in range(1, shards)]

    barrier = pltpu.get_barrier_semaphore()

    def greet(z, sh):
        pl.semaphore_signal(barrier, inc=1, device_id=where_is(z, sh), device_id_type=MESH)

    @pl.when(p >= 1)
    def _():
        greet(p - 1, me)

    @pl.when(p + 1 < pools)
    def _():
        greet(p + 1, me)

    for sh in peers:
        greet(p, sh)

    loads = [
        pltpu.make_async_copy(w_hbm.at[pl.ds(0, half)], w.at[pl.ds(0, half)], wsem.at[0]),
        pltpu.make_async_copy(w_hbm.at[pl.ds(half, half)], w.at[pl.ds(half, half)], wsem.at[1]),
        pltpu.make_async_copy(dn_hbm, dn, wsem.at[2]),
        pltpu.make_async_copy(up_hbm, up, wsem.at[3]),
        pltpu.make_async_copy(h_hbm, x.at[p, :, pl.ds(META, width)], wsem.at[4]),
    ]
    ic = pltpu.make_async_copy(idx_hbm, idx_ref, wsem.at[5])
    ic.start()
    for i in (4, 0, 2, 1, 3):
        loads[i].start()
    ic.wait()

    square = (rows_dev, rows_dev)
    down_axis = lax.broadcasted_iota(jnp.int32, square, 0)
    along = lax.broadcasted_iota(jnp.int32, square, 1)
    index = jnp.broadcast_to(idx_ref[...], square).astype(F32)
    column = jnp.sum(jnp.where(down_axis == along, index, 0.0), axis=1, keepdims=True)
    column = column.astype(jnp.int32)
    owner_column = column // stack
    first = lax.broadcasted_iota(jnp.int32, (rows_dev, META), 1) == 0
    meta = jnp.where(first, owner_column, column - owner_column * stack)
    x[p, :, pl.ds(0, META)] = meta.astype(F32).astype(BF16)

    greeters = jnp.minimum(p, 1) + jnp.minimum(pools - 1 - p, 1) + shards - 1
    pl.semaphore_wait(barrier, greeters)
    loads[4].wait()

    def piece(q):
        return pl.ds(META + q * part, part)

    def sent(q):
        return pl.ds(0, META + part) if q == 0 else piece(q)

    def to_right(b, q):
        ref = x.at[b, :, sent(q)]
        return rcopy(ref, ref, hright.at[b, q], hrecv.at[b, q], p + 1, me)

    def to_left(b, q):
        ref = x.at[b, :, sent(q)]
        return rcopy(ref, ref, hleft.at[b, q], hrecv.at[b, q], p - 1, me)

    for q in range(shards):
        @pl.when(p + 1 < pools)
        def _():
            to_right(p, q).start()

        @pl.when(p >= 1)
        def _():
            to_left(p, q).start()

    before = jnp.where(down_axis < along, 1.0, 0.0).astype(BF16)

    def selection(b):
        pick_owner = lax.broadcasted_iota(jnp.int32, (SLOTS, META), 1) == 0
        owner = lax.dot_general(
            jnp.where(pick_owner, 1.0, 0.0).astype(BF16), x[b, :, pl.ds(0, META)],
            (((1,), (1,)), ((), ())), preferred_element_type=F32,
        )
        owned = jnp.where(owner == p.astype(F32), 1.0, 0.0)
        rank = jnp.dot(owned.astype(BF16), before, preferred_element_type=F32)
        slot = lax.broadcasted_iota(jnp.int32, (SLOTS, rows_dev), 0).astype(F32)
        return jnp.where(rank == slot, owned, 0.0).astype(BF16)

    def pick(b, chosen, tag, q):
        got = jnp.dot(chosen, x[b, :, piece(q)], preferred_element_type=F32).astype(BF16)

        @pl.when(q != me)
        def _():
            picked[b, q, :, pl.ds(0, META)] = tag
            picked[b, q, :, pl.ds(META, part)] = got
            rcopy(picked.at[b, q], rows.at[b, me], rsend.at[b, q], rrecv.at[b, me], p, q).start()

        @pl.when(q == me)
        def _():
            rows[b, me, :, pl.ds(0, META)] = tag
            rows[b, me, :, pl.ds(META, part)] = got

    def select_tag(b):
        chosen = selection(b)
        tag = jnp.dot(chosen, x[b, :, pl.ds(0, META)], preferred_element_type=F32).astype(BF16)
        return chosen, tag

    def arrive(b, q, from_left):
        rcopy(
            x.at[b, :, sent(q)], x.at[b, :, sent(q)], hright.at[b, q], hrecv.at[b, q], p, peers[0]
        ).wait_recv()
        if from_left:
            @pl.when(p + 1 < pools)
            def _():
                to_right(b, q).start()
        else:
            @pl.when(p >= 1)
            def _():
                to_left(b, q).start()

    def receive(b, from_left):
        arrive(b, 0, from_left)
        chosen, tag = select_tag(b)
        pick(b, chosen, tag, 0)
        for q in range(1, shards):
            arrive(b, q, from_left)
            pick(b, chosen, tag, q)

    def project(b, k, last):
        tile = tile_of(cols)

        for j in range(cols // tile):
            at = pl.ds(j * tile, tile)
            term = jnp.dot(
                x[b, :, pl.ds(META + k * half, half)], w[pl.ds(k * half, half), at],
                preferred_element_type=F32,
            )
            if last:
                base[b, :, at] = (acc[b, :, at] + term).astype(BF16)
            else:
                acc[b, :, at] = term

    mine_cols = pl.ds(pl.multiple_of(p * cols, 128), cols)
    mine_slots = pl.ds(pl.multiple_of(p * SLOTS, SLOTS), SLOTS)

    def base_copy(b):
        return rcopy(base.at[b], home_base.at[:, mine_cols], bsend.at[b], brecv.at[p], b, me)

    def delta_copy(b, sh):
        return rcopy(
            delta.at[b, sh], home_delta.at[me, mine_slots], dsend.at[b, sh], drecv.at[p, me], b, sh
        )

    lane = lax.broadcasted_iota(jnp.int32, (many, 256), 1) // ranks
    lower = lax.broadcasted_iota(jnp.int32, (many // 2, 128), 1) < 64

    def adapter_of(b):
        tag = rows[b, :, :, pl.ds(0, META)].reshape(many, META).astype(F32)
        return tag[:, 1:2].astype(jnp.int32)

    def shrink(b):
        for sh in peers:
            rcopy(rows.at[b, sh], rows.at[b, sh], rsend.at[b, sh], rrecv.at[b, sh], p, sh).wait_recv()
        adapter = adapter_of(b)
        here = rows[b, :, :, pl.ds(META, part)].reshape(many, part)
        total = jnp.zeros((many, 128), F32)
        for j in range(tiles):
            term = lax.dot_general(
                here, dn[pl.ds(j * 256, 256), :], (((1,), (1,)), ((), ())),
                preferred_element_type=F32,
            )
            term = jnp.where(lane + j * each == adapter, term, 0.0)
            total = total + term[:, :128] + term[:, 128:]
        total = total + pltpu.roll(total, 64, 1)
        packed = jnp.where(lower, total[: many // 2], total[many // 2 :])
        low_out[b] = packed
        low[b, me] = packed
        for sh in peers:
            rcopy(low_out.at[b], low.at[b, me], lsend.at[b, sh], lrecv.at[b, me], p, sh).start()

    def grow(b):
        for sh in peers:
            rcopy(low_out.at[b], low.at[b, sh], lsend.at[b, sh], lrecv.at[b, sh], p, sh).wait_recv()
        adapter = adapter_of(b)
        both = low[b, 0]
        for sh in range(1, shards):
            both = both + low[b, sh]
        both = both.astype(BF16).astype(F32)
        turned = pltpu.roll(both, 64, 1)
        full = jnp.concatenate(
            [jnp.where(lower, both, turned), jnp.where(lower, turned, both)], axis=0
        )
        full = jnp.concatenate([full, full], axis=1)
        spread = jnp.concatenate(
            [
                jnp.where(lane + j * each == adapter, full, 0.0).astype(BF16)
                for j in range(tiles)
            ],
            axis=1,
        )
        rest = jnp.dot(spread, up[:, pl.ds(3 * quarter, quarter)], preferred_element_type=F32)
        top = lax.broadcasted_iota(jnp.int32, (many, quarter), 0) % SLOTS < HELD
        for j in range(3):
            at = pl.ds(j * quarter, quarter)
            term = jnp.dot(spread, up[:, at], preferred_element_type=F32)
            term = jnp.where(top, term, pltpu.roll(rest, HELD - 4 * j, 0))
            delta[b, :, :, at] = (ADAPTER_SCALE * term).astype(BF16).reshape(shards, SLOTS, quarter)
        for sh in range(shards):
            @pl.when(jnp.logical_or(b != p, sh != me))
            def _():
                delta_copy(b, sh).start()

            @pl.when(jnp.logical_and(b == p, sh == me))
            def _():
                home_delta[me, mine_slots] = delta[b, sh]

    def both_sides(t, f):
        def turn(i, c):
            b = jnp.where(i == 0, p - t, p + t)
            valid = jnp.logical_and(jnp.logical_and(b >= 0, b < pools), jnp.logical_or(i == 0, t > 0))

            @pl.when(valid)
            def _():
                f(b)
            return c

        lax.fori_loop(0, 2, turn, 0)

    chosen, tag = select_tag(p)
    for q in range(shards):
        pick(p, chosen, tag, q)

    def step(t, carry):
        @pl.when(t == 0)
        def _():
            loads[0].wait()
        both_sides(t, lambda b: project(b, 0, False))

        @pl.when(t == 0)
        def _():
            loads[2].wait()
        both_sides(t, shrink)

        @pl.when(t == 0)
        def _():
            loads[1].wait()

        def finish(b):
            project(b, 1, True)

            @pl.when(b != p)
            def _():
                base_copy(b).start()

            @pl.when(b == p)
            def _():
                home_base[:, mine_cols] = base[b]

        inner = jnp.logical_and(jnp.logical_and(p - t >= 0, p + t < pools), t > 0)

        def phase(i, c):
            @pl.when(i == jnp.where(inner, 1, 0))
            def _():
                both_sides(t, finish)

            @pl.when(i == jnp.where(inner, 0, 1))
            def _():
                @pl.when(p - 1 - t >= 0)
                def _():
                    receive(p - 1 - t, True)

                @pl.when(p + 1 + t < pools)
                def _():
                    receive(p + 1 + t, False)
            return c

        lax.fori_loop(0, 2, phase, 0)

        @pl.when(t == 0)
        def _():
            loads[3].wait()
        both_sides(t, grow)
        return carry

    lax.fori_loop(0, pools, step, 0)

    slots = pools * SLOTS
    lanes = lax.broadcasted_iota(jnp.int32, (rows_dev, slots), 1)
    owner = jnp.where(owner_column == lanes // SLOTS, 1.0, 0.0)
    after = jnp.where(down_axis > along, 1.0, 0.0).astype(BF16)
    rank = jnp.dot(after, owner.astype(BF16), preferred_element_type=F32)
    seat = lanes % SLOTS
    place = jnp.where(rank == seat.astype(F32), owner, 0.0).astype(BF16)
    tails = [
        jnp.where(
            jnp.logical_and(seat >= HELD, rank == (seat - HELD + 4 * k).astype(F32)), owner, 0.0
        ).astype(BF16)
        for k in range(3)
    ]

    places = jnp.concatenate([place] + tails, axis=0)

    def base_wait(z, carry):
        @pl.when(z != p)
        def _():
            dst = home_base.at[:, pl.ds(pl.multiple_of(z * cols, 128), cols)]
            rcopy(base.at[z], dst, bsend.at[z], brecv.at[z], z, me).wait_recv()
        return carry

    lax.fori_loop(0, pools, base_wait, 0)

    for sh in range(shards):
        def delta_wait(z, carry):
            @pl.when(jnp.logical_or(z != p, sh != me))
            def _():
                dst = home_delta.at[sh, pl.ds(pl.multiple_of(z * SLOTS, SLOTS), SLOTS)]
                rcopy(delta.at[z, sh], dst, dsend.at[z, sh], drecv.at[z, sh], z, sh).wait_recv()
            return carry

        lax.fori_loop(0, pools, delta_wait, 0)
        start = sh * part
        wide = 3 * quarter
        term = jnp.dot(places, home_delta[sh], preferred_element_type=F32)
        at = pl.ds(start, wide)
        out_ref[:, at] = (home_base[:, at].astype(F32) + term[:rows_dev]).astype(BF16)
        rest = term[rows_dev : 2 * rows_dev, :quarter]
        rest = rest + term[2 * rows_dev : 3 * rows_dev, quarter : 2 * quarter]
        rest = rest + term[3 * rows_dev :, 2 * quarter :]
        at = pl.ds(start + wide, quarter)
        out_ref[:, at] = (home_base[:, at].astype(F32) + rest).astype(BF16)

    def drain(b, carry):
        for q in range(shards):
            @pl.when(jnp.logical_and(b <= p, p + 1 < pools))
            def _():
                to_right(b, q).wait_send()

            @pl.when(jnp.logical_and(b >= p, p >= 1))
            def _():
                to_left(b, q).wait_send()

            @pl.when(q != me)
            def _():
                rcopy(picked.at[b, q], rows.at[b, me], rsend.at[b, q], rrecv.at[b, me], p, q).wait_send()
                rcopy(low_out.at[b], low.at[b, me], lsend.at[b, q], lrecv.at[b, me], p, q).wait_send()

            @pl.when(jnp.logical_or(b != p, q != me))
            def _():
                delta_copy(b, q).wait_send()

        @pl.when(b != p)
        def _():
            base_copy(b).wait_send()
        return carry

    lax.fori_loop(0, pools, drain, 0)


def local(hidden, query_weight_matrix, adapter_down_weight, adapter_up_weight, adapter_index_rows):
    pools = lax.axis_size("pool")
    chips = lax.axis_size("chip")
    shards = lax.axis_size("sub") * chips
    row_count, width = hidden.shape
    cols = query_weight_matrix.shape[1]
    stack, ranks, part = adapter_down_weight.shape
    if 2 + row_count // (pools - 1) > HELD:
        raise ValueError("owner overflow")
    dma = pltpu.SemaphoreType.DMA
    vmem = pl.BlockSpec(memory_space=pltpu.VMEM)
    hbm = pl.BlockSpec(memory_space=pl.ANY)
    return pl.pallas_call(
        functools.partial(kernel, pools, chips, shards, stack),
        out_shape=jax.ShapeDtypeStruct((row_count, width), BF16),
        in_specs=[hbm, hbm, hbm, hbm, hbm],
        out_specs=vmem,
        scratch_shapes=[
            pltpu.VMEM((pools, row_count, META + width), BF16),
            pltpu.VMEM((width, cols), BF16),
            pltpu.VMEM((stack * ranks, part), BF16),
            pltpu.VMEM((stack * ranks, part), BF16),
            pltpu.VMEM((pools, shards, SLOTS, META + part), BF16),
            pltpu.VMEM((pools, shards, SLOTS, META + part), BF16),
            pltpu.VMEM((pools, shards * SLOTS // 2, 128), F32),
            pltpu.VMEM((pools, shards, shards * SLOTS // 2, 128), F32),
            pltpu.VMEM((pools, shards, SLOTS, part - part // 4), BF16),
            pltpu.VMEM((shards, pools * SLOTS, part - part // 4), BF16),
            pltpu.VMEM((pools, row_count, cols), BF16),
            pltpu.VMEM((row_count, width), BF16),
            pltpu.VMEM((pools, row_count, cols), F32),
            pltpu.VMEM((1, row_count), jnp.int32),
            dma((6,)),
            dma((pools, shards)),
            dma((pools, shards)),
            dma((pools, shards)),
            dma((pools, shards)),
            dma((pools, shards)),
            dma((pools, shards)),
            dma((pools, shards)),
            dma((pools,)),
            dma((pools,)),
            dma((pools, shards)),
            dma((pools, shards)),
        ],
        compiler_params=pltpu.CompilerParams(
            collective_id=0, has_side_effects=True, vmem_limit_bytes=48 * 1024 * 1024
        ),
    )(
        *(
            pltpu.with_memory_space_constraint(array, pltpu.HBM)
            for array in (
                hidden,
                adapter_index_rows[None, :],
                query_weight_matrix,
                adapter_down_weight.reshape(stack * ranks, part),
                adapter_up_weight.reshape(stack * ranks, part),
            )
        )
    )


def solution(mesh):
    in_specs = (
        P(("groups", "pool", "sub", "chip"), None),
        P(None, "pool"),
        P("pool", None, ("sub", "chip")),
        P("pool", None, ("sub", "chip")),
        P(("groups", "pool", "sub", "chip")),
    )
    out_specs = P(("groups", "pool", "sub", "chip"), None)
    return jax.shard_map(local, mesh=mesh, in_specs=in_specs, out_specs=out_specs, check_vma=False)
```

```python
import functools

import jax
import jax.numpy as jnp
from jax import lax
from jax.experimental import pallas as pl
from jax.experimental.pallas import tpu as pltpu
from jax.sharding import PartitionSpec as P

ADAPTER_SCALE = 0.5
SLOTS = 16
HELD = 12
META = 128
MESH = pl.DeviceIdType.MESH
F32 = jnp.float32
BF16 = jnp.bfloat16


def tile_of(extent):
    return 256 if extent % 256 == 0 else extent


def kernel(
    pools, chips, shards, stack,
    h_hbm, idx_hbm, w_hbm, dn_hbm, up_hbm, out_ref,
    x, w, dn, up, picked, rows, low_out, low, delta, home_delta, base, home_base, acc,
    idx_ref, wsem, hright, hleft, hrecv, rsend, rrecv, lsend, lrecv, bsend, brecv, dsend, drecv,
):
    p = lax.axis_index("pool")
    me = lax.axis_index("sub") * chips + lax.axis_index("chip")
    rows_dev, width = h_hbm.shape
    cols = w.shape[1]
    part = width // shards
    half = width // 2
    quarter = part // 4
    ranks = dn.shape[0] // stack
    tiles = stack * ranks // 256
    each = 256 // ranks
    many = shards * SLOTS

    def where_is(z, sh):
        return {"pool": z, "sub": sh // chips, "chip": sh % chips}

    def rcopy(src, dst, ssem, rsem, z, sh):
        return pltpu.make_async_remote_copy(
            src_ref=src, dst_ref=dst, send_sem=ssem, recv_sem=rsem,
            device_id=where_is(z, sh), device_id_type=MESH,
        )

    peers = [(me + d) % shards for d in range(1, shards)]

    barrier = pltpu.get_barrier_semaphore()

    def greet(z, sh):
        pl.semaphore_signal(barrier, inc=1, device_id=where_is(z, sh), device_id_type=MESH)

    @pl.when(p >= 1)
    def _():
        greet(p - 1, me)

    @pl.when(p + 1 < pools)
    def _():
        greet(p + 1, me)

    for sh in peers:
        greet(p, sh)

    loads = [
        pltpu.make_async_copy(w_hbm.at[pl.ds(0, half)], w.at[pl.ds(0, half)], wsem.at[0]),
        pltpu.make_async_copy(w_hbm.at[pl.ds(half, half)], w.at[pl.ds(half, half)], wsem.at[1]),
        pltpu.make_async_copy(dn_hbm, dn, wsem.at[2]),
        pltpu.make_async_copy(up_hbm, up, wsem.at[3]),
        pltpu.make_async_copy(h_hbm, x.at[p, :, pl.ds(META, width)], wsem.at[4]),
    ]
    ic = pltpu.make_async_copy(idx_hbm, idx_ref, wsem.at[5])
    ic.start()
    for i in (4, 0, 2, 1, 3):
        loads[i].start()
    ic.wait()

    square = (rows_dev, rows_dev)
    down_axis = lax.broadcasted_iota(jnp.int32, square, 0)
    along = lax.broadcasted_iota(jnp.int32, square, 1)
    index = jnp.broadcast_to(idx_ref[...], square).astype(F32)
    column = jnp.sum(jnp.where(down_axis == along, index, 0.0), axis=1, keepdims=True)
    column = column.astype(jnp.int32)
    owner_column = column // stack
    first = lax.broadcasted_iota(jnp.int32, (rows_dev, META), 1) == 0
    meta = jnp.where(first, owner_column, column - owner_column * stack)
    x[p, :, pl.ds(0, META)] = meta.astype(F32).astype(BF16)

    greeters = jnp.minimum(p, 1) + jnp.minimum(pools - 1 - p, 1) + shards - 1
    pl.semaphore_wait(barrier, greeters)
    loads[4].wait()

    def piece(q):
        return pl.ds(META + q * part, part)

    def sent(q):
        return pl.ds(0, META + part) if q == 0 else piece(q)

    def to_right(b, q):
        ref = x.at[b, :, sent(q)]
        return rcopy(ref, ref, hright.at[b, q], hrecv.at[b, q], p + 1, me)

    def to_left(b, q):
        ref = x.at[b, :, sent(q)]
        return rcopy(ref, ref, hleft.at[b, q], hrecv.at[b, q], p - 1, me)

    for q in range(shards):
        @pl.when(p + 1 < pools)
        def _():
            to_right(p, q).start()

        @pl.when(p >= 1)
        def _():
            to_left(p, q).start()

    before = jnp.where(down_axis < along, 1.0, 0.0).astype(BF16)

    def selection(b):
        pick_owner = lax.broadcasted_iota(jnp.int32, (SLOTS, META), 1) == 0
        owner = lax.dot_general(
            jnp.where(pick_owner, 1.0, 0.0).astype(BF16), x[b, :, pl.ds(0, META)],
            (((1,), (1,)), ((), ())), preferred_element_type=F32,
        )
        owned = jnp.where(owner == p.astype(F32), 1.0, 0.0)
        rank = jnp.dot(owned.astype(BF16), before, preferred_element_type=F32)
        slot = lax.broadcasted_iota(jnp.int32, (SLOTS, rows_dev), 0).astype(F32)
        return jnp.where(rank == slot, owned, 0.0).astype(BF16)

    def pick(b, chosen, tag, q):
        got = jnp.dot(chosen, x[b, :, piece(q)], preferred_element_type=F32).astype(BF16)

        @pl.when(q != me)
        def _():
            picked[b, q, :, pl.ds(0, META)] = tag
            picked[b, q, :, pl.ds(META, part)] = got
            rcopy(picked.at[b, q], rows.at[b, me], rsend.at[b, q], rrecv.at[b, me], p, q).start()

        @pl.when(q == me)
        def _():
            rows[b, me, :, pl.ds(0, META)] = tag
            rows[b, me, :, pl.ds(META, part)] = got

    def select_tag(b):
        chosen = selection(b)
        tag = jnp.dot(chosen, x[b, :, pl.ds(0, META)], preferred_element_type=F32).astype(BF16)
        return chosen, tag

    def arrive(b, q, from_left):
        rcopy(
            x.at[b, :, sent(q)], x.at[b, :, sent(q)], hright.at[b, q], hrecv.at[b, q], p, peers[0]
        ).wait_recv()
        if from_left:
            @pl.when(p + 1 < pools)
            def _():
                to_right(b, q).start()
        else:
            @pl.when(p >= 1)
            def _():
                to_left(b, q).start()

    def receive(b, from_left):
        arrive(b, 0, from_left)
        chosen, tag = select_tag(b)
        pick(b, chosen, tag, 0)
        for q in range(1, shards):
            arrive(b, q, from_left)
            pick(b, chosen, tag, q)

    def project(b, k, last):
        tile = tile_of(cols)

        for j in range(cols // tile):
            at = pl.ds(j * tile, tile)
            term = jnp.dot(
                x[b, :, pl.ds(META + k * half, half)], w[pl.ds(k * half, half), at],
                preferred_element_type=F32,
            )
            if last:
                base[b, :, at] = (acc[b, :, at] + term).astype(BF16)
            else:
                acc[b, :, at] = term

    mine_cols = pl.ds(pl.multiple_of(p * cols, 128), cols)
    mine_slots = pl.ds(pl.multiple_of(p * SLOTS, SLOTS), SLOTS)

    def base_copy(b):
        return rcopy(base.at[b], home_base.at[:, mine_cols], bsend.at[b], brecv.at[p], b, me)

    def delta_copy(b, sh):
        return rcopy(
            delta.at[b, sh], home_delta.at[me, mine_slots], dsend.at[b, sh], drecv.at[p, me], b, sh
        )

    lane = lax.broadcasted_iota(jnp.int32, (many, 256), 1) // ranks
    lower = lax.broadcasted_iota(jnp.int32, (many // 2, 128), 1) < 64

    def adapter_of(b):
        tag = rows[b, :, :, pl.ds(0, META)].reshape(many, META).astype(F32)
        return tag[:, 1:2].astype(jnp.int32)

    def shrink(b):
        for sh in peers:
            rcopy(rows.at[b, sh], rows.at[b, sh], rsend.at[b, sh], rrecv.at[b, sh], p, sh).wait_recv()
        adapter = adapter_of(b)
        here = rows[b, :, :, pl.ds(META, part)].reshape(many, part)
        total = jnp.zeros((many, 128), F32)
        for j in range(tiles):
            term = lax.dot_general(
                here, dn[pl.ds(j * 256, 256), :], (((1,), (1,)), ((), ())),
                preferred_element_type=F32,
            )
            term = jnp.where(lane + j * each == adapter, term, 0.0)
            total = total + term[:, :128] + term[:, 128:]
        total = total + pltpu.roll(total, 64, 1)
        packed = jnp.where(lower, total[: many // 2], total[many // 2 :])
        low_out[b] = packed
        low[b, me] = packed
        for sh in peers:
            rcopy(low_out.at[b], low.at[b, me], lsend.at[b, sh], lrecv.at[b, me], p, sh).start()

    def grow(b):
        for sh in peers:
            rcopy(low_out.at[b], low.at[b, sh], lsend.at[b, sh], lrecv.at[b, sh], p, sh).wait_recv()
        adapter = adapter_of(b)
        both = low[b, 0]
        for sh in range(1, shards):
            both = both + low[b, sh]
        both = both.astype(BF16).astype(F32)
        turned = pltpu.roll(both, 64, 1)
        full = jnp.concatenate(
            [jnp.where(lower, both, turned), jnp.where(lower, turned, both)], axis=0
        )
        full = jnp.concatenate([full, full], axis=1)
        spread = jnp.concatenate(
            [
                jnp.where(lane + j * each == adapter, full, 0.0).astype(BF16)
                for j in range(tiles)
            ],
            axis=1,
        )
        rest = jnp.dot(spread, up[:, pl.ds(3 * quarter, quarter)], preferred_element_type=F32)
        top = lax.broadcasted_iota(jnp.int32, (many, quarter), 0) % SLOTS < HELD
        for j in range(3):
            at = pl.ds(j * quarter, quarter)
            term = jnp.dot(spread, up[:, at], preferred_element_type=F32)
            term = jnp.where(top, term, pltpu.roll(rest, HELD - 4 * j, 0))
            delta[b, :, :, at] = (ADAPTER_SCALE * term).astype(BF16).reshape(shards, SLOTS, quarter)
        for sh in range(shards):
            @pl.when(jnp.logical_or(b != p, sh != me))
            def _():
                delta_copy(b, sh).start()

            @pl.when(jnp.logical_and(b == p, sh == me))
            def _():
                home_delta[me, mine_slots] = delta[b, sh]

    def both_sides(t, f):
        def turn(i, c):
            b = jnp.where((i == 0) == (2 * p < pools), p + t, p - t)
            valid = jnp.logical_and(jnp.logical_and(b >= 0, b < pools), jnp.logical_or(i == 0, t > 0))

            @pl.when(valid)
            def _():
                f(b)
            return c

        lax.fori_loop(0, 2, turn, 0)

    chosen, tag = select_tag(p)
    for q in range(shards):
        pick(p, chosen, tag, q)

    def step(t, carry):
        @pl.when(t == 0)
        def _():
            loads[0].wait()
        both_sides(t, lambda b: project(b, 0, False))

        @pl.when(t == 0)
        def _():
            loads[2].wait()
        both_sides(t, shrink)

        @pl.when(t == 0)
        def _():
            loads[1].wait()

        def finish(b):
            project(b, 1, True)

            @pl.when(b != p)
            def _():
                base_copy(b).start()

            @pl.when(b == p)
            def _():
                home_base[:, mine_cols] = base[b]

        inner = jnp.logical_and(jnp.logical_and(p - t >= 0, p + t < pools), t > 0)

        def phase(i, c):
            @pl.when(i == jnp.where(inner, 1, 0))
            def _():
                both_sides(t, finish)

            @pl.when(i == jnp.where(inner, 0, 1))
            def _():
                def side(i, c):
                    from_right = (i == 0) == (p < 0)

                    @pl.when(jnp.logical_and(jnp.logical_not(from_right), p - 1 - t >= 0))
                    def _():
                        receive(p - 1 - t, True)

                    @pl.when(jnp.logical_and(from_right, p + 1 + t < pools))
                    def _():
                        receive(p + 1 + t, False)
                    return c

                lax.fori_loop(0, 2, side, 0)
            return c

        lax.fori_loop(0, 2, phase, 0)

        @pl.when(t == 0)
        def _():
            loads[3].wait()
        both_sides(t, grow)
        return carry

    lax.fori_loop(0, pools, step, 0)

    slots = pools * SLOTS
    lanes = lax.broadcasted_iota(jnp.int32, (rows_dev, slots), 1)
    owner = jnp.where(owner_column == lanes // SLOTS, 1.0, 0.0)
    after = jnp.where(down_axis > along, 1.0, 0.0).astype(BF16)
    rank = jnp.dot(after, owner.astype(BF16), preferred_element_type=F32)
    seat = lanes % SLOTS
    place = jnp.where(rank == seat.astype(F32), owner, 0.0).astype(BF16)
    tails = [
        jnp.where(
            jnp.logical_and(seat >= HELD, rank == (seat - HELD + 4 * k).astype(F32)), owner, 0.0
        ).astype(BF16)
        for k in range(3)
    ]

    places = jnp.concatenate([place] + tails, axis=0)

    def base_wait(z, carry):
        @pl.when(z != p)
        def _():
            dst = home_base.at[:, pl.ds(pl.multiple_of(z * cols, 128), cols)]
            rcopy(base.at[z], dst, bsend.at[z], brecv.at[z], z, me).wait_recv()
        return carry

    lax.fori_loop(0, pools, base_wait, 0)

    for sh in range(shards):
        def delta_wait(z, carry):
            @pl.when(jnp.logical_or(z != p, sh != me))
            def _():
                dst = home_delta.at[sh, pl.ds(pl.multiple_of(z * SLOTS, SLOTS), SLOTS)]
                rcopy(delta.at[z, sh], dst, dsend.at[z, sh], drecv.at[z, sh], z, sh).wait_recv()
            return carry

        lax.fori_loop(0, pools, delta_wait, 0)
        start = sh * part
        wide = 3 * quarter
        term = jnp.dot(places, home_delta[sh], preferred_element_type=F32)
        at = pl.ds(start, wide)
        out_ref[:, at] = (home_base[:, at].astype(F32) + term[:rows_dev]).astype(BF16)
        rest = term[rows_dev : 2 * rows_dev, :quarter]
        rest = rest + term[2 * rows_dev : 3 * rows_dev, quarter : 2 * quarter]
        rest = rest + term[3 * rows_dev :, 2 * quarter :]
        at = pl.ds(start + wide, quarter)
        out_ref[:, at] = (home_base[:, at].astype(F32) + rest).astype(BF16)

    def drain(b, carry):
        for q in range(shards):
            @pl.when(jnp.logical_and(b <= p, p + 1 < pools))
            def _():
                to_right(b, q).wait_send()

            @pl.when(jnp.logical_and(b >= p, p >= 1))
            def _():
                to_left(b, q).wait_send()

            @pl.when(q != me)
            def _():
                rcopy(picked.at[b, q], rows.at[b, me], rsend.at[b, q], rrecv.at[b, me], p, q).wait_send()
                rcopy(low_out.at[b], low.at[b, me], lsend.at[b, q], lrecv.at[b, me], p, q).wait_send()

            @pl.when(jnp.logical_or(b != p, q != me))
            def _():
                delta_copy(b, q).wait_send()

        @pl.when(b != p)
        def _():
            base_copy(b).wait_send()
        return carry

    lax.fori_loop(0, pools, drain, 0)


def local(hidden, query_weight_matrix, adapter_down_weight, adapter_up_weight, adapter_index_rows):
    pools = lax.axis_size("pool")
    chips = lax.axis_size("chip")
    shards = lax.axis_size("sub") * chips
    row_count, width = hidden.shape
    cols = query_weight_matrix.shape[1]
    stack, ranks, part = adapter_down_weight.shape
    if 2 + row_count // (pools - 1) > HELD:
        raise ValueError("owner overflow")
    dma = pltpu.SemaphoreType.DMA
    vmem = pl.BlockSpec(memory_space=pltpu.VMEM)
    hbm = pl.BlockSpec(memory_space=pl.ANY)
    return pl.pallas_call(
        functools.partial(kernel, pools, chips, shards, stack),
        out_shape=jax.ShapeDtypeStruct((row_count, width), BF16),
        in_specs=[hbm, hbm, hbm, hbm, hbm],
        out_specs=vmem,
        scratch_shapes=[
            pltpu.VMEM((pools, row_count, META + width), BF16),
            pltpu.VMEM((width, cols), BF16),
            pltpu.VMEM((stack * ranks, part), BF16),
            pltpu.VMEM((stack * ranks, part), BF16),
            pltpu.VMEM((pools, shards, SLOTS, META + part), BF16),
            pltpu.VMEM((pools, shards, SLOTS, META + part), BF16),
            pltpu.VMEM((pools, shards * SLOTS // 2, 128), F32),
            pltpu.VMEM((pools, shards, shards * SLOTS // 2, 128), F32),
            pltpu.VMEM((pools, shards, SLOTS, part - part // 4), BF16),
            pltpu.VMEM((shards, pools * SLOTS, part - part // 4), BF16),
            pltpu.VMEM((pools, row_count, cols), BF16),
            pltpu.VMEM((row_count, width), BF16),
            pltpu.VMEM((pools, row_count, cols), F32),
            pltpu.VMEM((1, row_count), jnp.int32),
            dma((6,)),
            dma((pools, shards)),
            dma((pools, shards)),
            dma((pools, shards)),
            dma((pools, shards)),
            dma((pools, shards)),
            dma((pools, shards)),
            dma((pools, shards)),
            dma((pools,)),
            dma((pools,)),
            dma((pools, shards)),
            dma((pools, shards)),
        ],
        compiler_params=pltpu.CompilerParams(
            collective_id=0, has_side_effects=True, vmem_limit_bytes=48 * 1024 * 1024
        ),
    )(
        *(
            pltpu.with_memory_space_constraint(array, pltpu.HBM)
            for array in (
                hidden,
                adapter_index_rows[None, :],
                query_weight_matrix,
                adapter_down_weight.reshape(stack * ranks, part),
                adapter_up_weight.reshape(stack * ranks, part),
            )
        )
    )


def solution(mesh):
    in_specs = (
        P(("groups", "pool", "sub", "chip"), None),
        P(None, "pool"),
        P("pool", None, ("sub", "chip")),
        P("pool", None, ("sub", "chip")),
        P(("groups", "pool", "sub", "chip")),
    )
    out_specs = P(("groups", "pool", "sub", "chip"), None)
    return jax.shard_map(local, mesh=mesh, in_specs=in_specs, out_specs=out_specs, check_vma=False)
```

```python
import functools

import jax
import jax.numpy as jnp
from jax import lax
from jax.experimental import pallas as pl
from jax.experimental.pallas import tpu as pltpu
from jax.sharding import PartitionSpec as P

ADAPTER_SCALE = 0.5
SLOTS = 16
HELD = 12
META = 128
PIECES = 4
MESH = pl.DeviceIdType.MESH
F32 = jnp.float32
BF16 = jnp.bfloat16


def tile_of(extent):
    return 256 if extent % 256 == 0 else extent


def kernel(
    pools, chips, shards, stack,
    h_hbm, idx_hbm, w_hbm, dn_hbm, up_hbm, out_ref,
    x, xi, own, w, dn, up, chosen, chosen_part, tags, picked, rows, low_out, low, delta, home_delta, base, home_base, acc,
    idx_ref, wsem, hright, hleft, hrecv, rsend, rrecv, lsend, lrecv, bsend, brecv, dsend, drecv,
):
    p = lax.axis_index("pool")
    me = lax.axis_index("sub") * chips + lax.axis_index("chip")
    rows_dev, width = h_hbm.shape
    cols = w.shape[1]
    part = width // shards
    half = width // 2
    quarter = part // 4
    ranks = dn.shape[0] // stack
    tiles = stack * ranks // 256
    each = 256 // ranks
    many = shards * SLOTS

    def where_is(z, sh):
        return {"pool": z, "sub": sh // chips, "chip": sh % chips}

    def rcopy(src, dst, ssem, rsem, z, sh):
        return pltpu.make_async_remote_copy(
            src_ref=src, dst_ref=dst, send_sem=ssem, recv_sem=rsem,
            device_id=where_is(z, sh), device_id_type=MESH,
        )

    peers = [(me + d) % shards for d in range(1, shards)]

    barrier = pltpu.get_barrier_semaphore()

    def greet(z, sh):
        pl.semaphore_signal(barrier, inc=1, device_id=where_is(z, sh), device_id_type=MESH)

    @pl.when(p >= 1)
    def _():
        greet(p - 1, me)

    @pl.when(p + 1 < pools)
    def _():
        greet(p + 1, me)

    for sh in peers:
        greet(p, sh)

    loads = [
        pltpu.make_async_copy(w_hbm.at[pl.ds(0, half)], w.at[pl.ds(0, half)], wsem.at[0]),
        pltpu.make_async_copy(w_hbm.at[pl.ds(half, half)], w.at[pl.ds(half, half)], wsem.at[1]),
        pltpu.make_async_copy(dn_hbm, dn, wsem.at[2]),
        pltpu.make_async_copy(up_hbm, up, wsem.at[3]),
        pltpu.make_async_copy(h_hbm, own, wsem.at[4]),
    ]
    ic = pltpu.make_async_copy(idx_hbm, idx_ref, wsem.at[5])
    ic.start()
    for i in (4, 0, 2, 1, 3):
        loads[i].start()
    ic.wait()

    square = (rows_dev, rows_dev)
    down_axis = lax.broadcasted_iota(jnp.int32, square, 0)
    along = lax.broadcasted_iota(jnp.int32, square, 1)
    index = jnp.broadcast_to(idx_ref[...], square).astype(F32)
    column = jnp.sum(jnp.where(down_axis == along, index, 0.0), axis=1, keepdims=True)
    column = column.astype(jnp.int32)
    owner_column = column // stack
    row_owner = jnp.broadcast_to(idx_ref[...] // stack, square)
    col_owner = jnp.broadcast_to(owner_column, square)
    same = row_owner == col_owner
    ahead = jnp.logical_or(col_owner < row_owner, jnp.logical_and(same, down_axis < along))
    seat_row = jnp.sum(jnp.where(ahead, 1.0, 0.0), axis=0, keepdims=True)
    behind = jnp.logical_or(row_owner < col_owner, jnp.logical_and(same, along < down_axis))
    seat_column = jnp.sum(jnp.where(behind, 1.0, 0.0), axis=1, keepdims=True)
    to_sorted = jnp.where(seat_row == down_axis.astype(F32), 1.0, 0.0).astype(BF16)
    from_sorted = jnp.where(seat_column == along.astype(F32), 1.0, 0.0).astype(BF16)
    lane_index = lax.broadcasted_iota(jnp.int32, (rows_dev, META), 1).astype(F32)
    sorted_index = jnp.where(seat_column == lane_index, column.astype(F32), 0.0)
    xi[p] = jnp.sum(sorted_index, axis=0, keepdims=True).astype(jnp.int32)

    greeters = jnp.minimum(p, 1) + jnp.minimum(pools - 1 - p, 1) + shards - 1
    loads[4].wait()
    for q in range(shards):
        x[p, :, pl.ds(q * part, part)] = jnp.dot(
            to_sorted, own[:, pl.ds(q * part, part)], preferred_element_type=F32
        ).astype(BF16)
    pl.semaphore_wait(barrier, greeters)

    four = pools == 4 and shards == 4
    inner = jnp.logical_and(p >= 1, p + 1 < pools)
    even = p % 2 == 0
    half_rows = rows_dev // 2

    def order(k):
        if four:
            pair = jnp.where(even, p + 1, p - 1)
            second = jnp.where(p < 2, 2, 1)
            third = jnp.where(p < 2, 3, 0)
            return jnp.where(k == 0, p, jnp.where(k == 1, pair, jnp.where(k == 2, second, third)))
        both = jnp.minimum(p, pools - 1 - p)
        near = jnp.where(k % 2 == 1, (k + 1) // 2, -((k + 1) // 2))
        away = jnp.where(p <= pools - 1 - p, k - both, both - k)
        return p + jnp.where(k <= 2 * both, near, away)

    def quarter_of(q):
        return pl.ds(pl.multiple_of(q * part, 128), part)

    def lanes_of(f):
        return pl.ds(f * half, half)

    def to_right(b, i, row, f):
        ref = x.at[b, pl.ds(row, half_rows), lanes_of(f)]
        return rcopy(ref, ref, hright.at[b, i], hrecv.at[b, i], p + 1, me)

    def to_left(b, i, row, f):
        ref = x.at[b, pl.ds(row, half_rows), lanes_of(f)]
        return rcopy(ref, ref, hleft.at[b, i], hrecv.at[b, i], p - 1, me)

    def index_right(b):
        return rcopy(
            xi.at[b], xi.at[b], hright.at[b, PIECES], hrecv.at[b, PIECES], p + 1, me
        )

    def index_left(b):
        return rcopy(
            xi.at[b], xi.at[b], hleft.at[b, PIECES], hrecv.at[b, PIECES], p - 1, me
        )

    def own_right(i):
        return to_right(p, i, half_rows * (1 - i // 2), i % 2)

    def own_left(i):
        return to_left(p, i, half_rows * (i // 2), i % 2)

    @pl.when(p + 1 < pools)
    def _():
        index_right(p).start()

    @pl.when(p >= 1)
    def _():
        index_left(p).start()

    for i in range(PIECES):
        @pl.when(p + 1 < pools)
        def _():
            own_right(i).start()

        @pl.when(p >= 1)
        def _():
            own_left(i).start()

    before = jnp.where(down_axis < along, 1.0, 0.0).astype(BF16)

    def selection(b):
        index = xi[b][:, :rows_dev]
        held_by = index // stack
        local_index = (index - held_by * stack).astype(F32)
        spread_over = (SLOTS, rows_dev)
        owned = jnp.where(jnp.broadcast_to(held_by, spread_over) == p, 1.0, 0.0)
        rank = jnp.dot(owned.astype(BF16), before, preferred_element_type=F32)
        slot = lax.broadcasted_iota(jnp.int32, spread_over, 0).astype(F32)
        taken = jnp.where(rank == slot, owned, 0.0)
        tag = jnp.sum(taken * local_index, axis=1, keepdims=True)
        tags[b] = jnp.broadcast_to(tag, (SLOTS, META)).astype(BF16)
        return taken

    def place_pick(b, q, got):
        got = got.astype(BF16)

        @pl.when(q != me)
        def _():
            picked[b, q, :, pl.ds(0, META)] = tags[b]
            picked[b, q, :, pl.ds(META, part)] = got
            rcopy(picked.at[b, q], rows.at[b, me], rsend.at[b, q], rrecv.at[b, me], p, q).start()

        @pl.when(q == me)
        def _():
            rows[b, me, :, pl.ds(0, META)] = tags[b]
            rows[b, me, :, pl.ds(META, part)] = got

    def pick(b, q):
        place_pick(b, q, jnp.dot(chosen[b], x[b, :, quarter_of(q)], preferred_element_type=F32))

    def pick_part(b, q, at):
        place_pick(
            b, q, jnp.dot(chosen_part[b], x[b, at, quarter_of(q)], preferred_element_type=F32)
        )

    def table(at, values):
        value = values[0]
        for i in range(1, len(values)):
            value = jnp.where(at == i, values[i], value)
        return value

    if four:
        mid_seq = ((1, 0), (2, 0), (1, 1), (2, 1), (2, 2), (1, 2), (2, 3), (1, 3), (3, 0), (3, 1), (3, 2), (3, 3))
        end_seq = ((1, 0), (1, 1), (1, 2), (2, 0), (2, 1), (1, 3), (2, 2), (3, 0), (3, 1), (2, 3), (3, 2), (3, 3))
        arrivals = [
            jnp.where(inner, PIECES * a + b, PIECES * c + d)
            for (a, b), (c, d) in zip(mid_seq, end_seq)
        ]

    def receive(r, carry):
        at = table(r, arrivals) if four else PIECES + r
        k = at // PIECES
        i = at % PIECES
        b = order(k)
        phase = i // 2
        rightward = b < p
        row = pl.multiple_of(half_rows * jnp.where(rightward, 1 - phase, phase), half_rows)
        @pl.when(i == 0)
        def _():
            rcopy(
                xi.at[b], xi.at[b], hright.at[b, PIECES], hrecv.at[b, PIECES], p, peers[0]
            ).wait_recv()

            @pl.when(jnp.logical_and(rightward, p + 1 < pools))
            def _():
                index_right(b).start()

            @pl.when(jnp.logical_and(jnp.logical_not(rightward), p >= 1))
            def _():
                index_left(b).start()

        for f in range(2):
            @pl.when(i % 2 == f)
            def _():
                ref = x.at[b, pl.ds(row, half_rows), lanes_of(f)]
                rcopy(ref, ref, hright.at[b, i], hrecv.at[b, i], p, peers[0]).wait_recv()

                @pl.when(jnp.logical_and(rightward, p + 1 < pools))
                def _():
                    to_right(b, i, row, f).start()

                @pl.when(jnp.logical_and(jnp.logical_not(rightward), p >= 1))
                def _():
                    to_left(b, i, row, f).start()

        first_q = (i % 2) * (shards // 2)

        @pl.when(jnp.logical_and(inner, phase == 1))
        def _():
            @pl.when(i % 2 == 0)
            def _():
                chosen[b] = selection(b).astype(BF16)

            def one(q, c):
                pick(b, first_q + q)
                return c

            lax.fori_loop(0, shards // 2, one, 0)

        @pl.when(jnp.logical_and(jnp.logical_not(inner), phase == 0))
        def _():
            part_rows = pl.ds(row, half_rows)

            @pl.when(i % 2 == 0)
            def _():
                taken = selection(b)
                kept = jnp.where(row > 0, taken[:, half_rows:], taken[:, :half_rows])
                chosen_part[b] = kept.astype(BF16)

            def one(q, c):
                pick_part(b, first_q + q, part_rows)
                return c

            lax.fori_loop(0, shards // 2, one, 0)
        return carry

    def project(b, k, last):
        tile = tile_of(cols)

        for j in range(cols // tile):
            at = pl.ds(j * tile, tile)
            term = jnp.dot(
                x[b, :, pl.ds(k * half, half)], w[pl.ds(k * half, half), at],
                preferred_element_type=F32,
            )
            if last:
                base[b, :, at] = (acc[:, at] + term).astype(BF16)
            else:
                acc[:, at] = term

    mine_cols = pl.ds(pl.multiple_of(p * cols, 128), cols)
    mine_slots = pl.ds(pl.multiple_of(p * SLOTS, SLOTS), SLOTS)

    def base_copy(b):
        return rcopy(base.at[b], home_base.at[:, mine_cols], bsend.at[b], brecv.at[p], b, me)

    def delta_copy(b, sh):
        return rcopy(
            delta.at[b, sh], home_delta.at[me, mine_slots], dsend.at[b, sh], drecv.at[p, me], b, sh
        )

    lane = lax.broadcasted_iota(jnp.int32, (many, 256), 1) // ranks
    lower = lax.broadcasted_iota(jnp.int32, (many // 2, 128), 1) < 64

    def adapter_of(b):
        tag = rows[b, :, :, pl.ds(0, META)].reshape(many, META).astype(F32)
        return tag[:, 1:2].astype(jnp.int32)

    def shrink(b):
        for sh in peers:
            rcopy(rows.at[b, sh], rows.at[b, sh], rsend.at[b, sh], rrecv.at[b, sh], p, sh).wait_recv()
        adapter = adapter_of(b)
        here = rows[b, :, :, pl.ds(META, part)].reshape(many, part)
        total = jnp.zeros((many, 128), F32)
        for j in range(tiles):
            term = lax.dot_general(
                here, dn[pl.ds(j * 256, 256), :], (((1,), (1,)), ((), ())),
                preferred_element_type=F32,
            )
            term = jnp.where(lane + j * each == adapter, term, 0.0)
            total = total + term[:, :128] + term[:, 128:]
        total = total + pltpu.roll(total, 64, 1)
        packed = jnp.where(lower, total[: many // 2], total[many // 2 :])
        low_out[b] = packed
        low[b, me] = packed
        for sh in peers:
            rcopy(low_out.at[b], low.at[b, me], lsend.at[b, sh], lrecv.at[b, me], p, sh).start()

    def grow(b):
        for sh in peers:
            rcopy(low_out.at[b], low.at[b, sh], lsend.at[b, sh], lrecv.at[b, sh], p, sh).wait_recv()
        adapter = adapter_of(b)
        both = low[b, 0]
        for sh in range(1, shards):
            both = both + low[b, sh]
        both = both.astype(BF16).astype(F32)
        turned = pltpu.roll(both, 64, 1)
        full = jnp.concatenate(
            [jnp.where(lower, both, turned), jnp.where(lower, turned, both)], axis=0
        )
        full = jnp.concatenate([full, full], axis=1)
        spread = jnp.concatenate(
            [
                jnp.where(lane + j * each == adapter, full, 0.0).astype(BF16)
                for j in range(tiles)
            ],
            axis=1,
        )
        rest = jnp.dot(spread, up[:, pl.ds(3 * quarter, quarter)], preferred_element_type=F32)
        top = lax.broadcasted_iota(jnp.int32, (many, quarter), 0) % SLOTS < HELD
        for j in range(3):
            at = pl.ds(j * quarter, quarter)
            term = jnp.dot(spread, up[:, at], preferred_element_type=F32)
            term = jnp.where(top, term, pltpu.roll(rest, HELD - 4 * j, 0))
            delta[b, :, :, at] = (ADAPTER_SCALE * term).astype(BF16).reshape(shards, SLOTS, quarter)

    def give(b):
        for sh in range(shards):
            @pl.when(jnp.logical_or(b != p, sh != me))
            def _():
                delta_copy(b, sh).start()

            @pl.when(jnp.logical_and(b == p, sh == me))
            def _():
                home_delta[me, mine_slots] = delta[b, sh]

    def give_base(b):
        @pl.when(b != p)
        def _():
            base_copy(b).start()

        @pl.when(b == p)
        def _():
            home_base[:, mine_cols] = base[b]

    chosen[p] = selection(p).astype(BF16)

    def own_pick(q, c):
        pick(p, q)
        return c

    lax.fori_loop(0, shards, own_pick, 0)

    PA, S, PB, G = range(4)
    if four:
        mid_plan = ((0, PA, 0), (0, S, 0), (0, PB, 4), (2, PA, 8), (2, PB, 8), (2, S, 9), (3, PA, 11), (0, G, 12), (2, G, 12), (3, PB, 12), (3, S, 12), (1, S, 12), (1, PA, 12), (1, PB, 12), (3, G, 12), (1, G, 12))
        end_plan = ((0, PA, 0), (0, S, 0), (0, PB, 0), (0, G, 2), (1, S, 4), (1, PA, 4), (1, PB, 6), (2, S, 6), (1, G, 7), (2, G, 9), (2, PA, 10), (2, PB, 12), (3, S, 12), (3, PA, 12), (3, PB, 12), (3, G, 12))
        plan = [
            jnp.where(inner, 256 * d + 16 * a + b, 256 * g + 16 * e + f)
            for (a, b, d), (e, f, g) in zip(mid_plan, end_plan)
        ]

    def chunk(c, done):
        if four:
            at = table(c, plan)
            ready = at // 256
            k = (at // 16) % 16
            j = at % 16
        else:
            ready = PIECES * (c // 4)
            k = c // 4
            j = c % 4
        lax.fori_loop(done, ready, receive, 0)
        b = order(k)

        @pl.when(j == PA)
        def _():
            @pl.when(k == 0)
            def _():
                loads[0].wait()
            project(b, 0, False)

        @pl.when(j == S)
        def _():
            @pl.when(k == 0)
            def _():
                loads[2].wait()
            shrink(b)

        @pl.when(j == PB)
        def _():
            @pl.when(k == 0)
            def _():
                loads[1].wait()
            project(b, 1, True)
            give_base(b)

        @pl.when(j == G)
        def _():
            @pl.when(k == 0)
            def _():
                loads[3].wait()
            grow(b)
            give(b)
        return ready

    lax.fori_loop(0, 4 * pools, chunk, 0)

    slots = pools * SLOTS
    lanes = lax.broadcasted_iota(jnp.int32, (rows_dev, slots), 1)
    owner = jnp.where(owner_column == lanes // SLOTS, 1.0, 0.0)
    after = jnp.where(down_axis > along, 1.0, 0.0).astype(BF16)
    rank = jnp.dot(after, owner.astype(BF16), preferred_element_type=F32)
    seat = lanes % SLOTS
    place = jnp.where(rank == seat.astype(F32), owner, 0.0).astype(BF16)
    tails = [
        jnp.where(
            jnp.logical_and(seat >= HELD, rank == (seat - HELD + 4 * k).astype(F32)), owner, 0.0
        ).astype(BF16)
        for k in range(3)
    ]

    places = jnp.concatenate([place] + tails, axis=0)

    def base_wait(z, carry):
        @pl.when(z != p)
        def _():
            dst = home_base.at[:, pl.ds(pl.multiple_of(z * cols, 128), cols)]
            rcopy(base.at[z], dst, bsend.at[z], brecv.at[z], z, me).wait_recv()
        return carry

    lax.fori_loop(0, pools, base_wait, 0)

    def mine(at):
        return jnp.dot(from_sorted, home_base[:, at], preferred_element_type=F32)

    for sh in range(shards):
        def delta_wait(z, carry):
            @pl.when(jnp.logical_or(z != p, sh != me))
            def _():
                dst = home_delta.at[sh, pl.ds(pl.multiple_of(z * SLOTS, SLOTS), SLOTS)]
                rcopy(delta.at[z, sh], dst, dsend.at[z, sh], drecv.at[z, sh], z, sh).wait_recv()
            return carry

        lax.fori_loop(0, pools, delta_wait, 0)
        start = sh * part
        wide = 3 * quarter
        term = jnp.dot(places, home_delta[sh], preferred_element_type=F32)
        at = pl.ds(start, wide)
        out_ref[:, at] = (mine(at) + term[:rows_dev]).astype(BF16)
        rest = term[rows_dev : 2 * rows_dev, :quarter]
        rest = rest + term[2 * rows_dev : 3 * rows_dev, quarter : 2 * quarter]
        rest = rest + term[3 * rows_dev :, 2 * quarter :]
        at = pl.ds(start + wide, quarter)
        out_ref[:, at] = (mine(at) + rest).astype(BF16)

    def drain(b, carry):
        @pl.when(jnp.logical_and(b <= p, p + 1 < pools))
        def _():
            index_right(b).wait_send()

        @pl.when(jnp.logical_and(b >= p, p >= 1))
        def _():
            index_left(b).wait_send()

        for i in range(PIECES):
            @pl.when(jnp.logical_and(b <= p, p + 1 < pools))
            def _():
                to_right(b, i, half_rows * (1 - i // 2), i % 2).wait_send()

            @pl.when(jnp.logical_and(b >= p, p >= 1))
            def _():
                to_left(b, i, half_rows * (i // 2), i % 2).wait_send()

        for q in range(shards):
            @pl.when(q != me)
            def _():
                rcopy(picked.at[b, q], rows.at[b, me], rsend.at[b, q], rrecv.at[b, me], p, q).wait_send()
                rcopy(low_out.at[b], low.at[b, me], lsend.at[b, q], lrecv.at[b, me], p, q).wait_send()

            @pl.when(jnp.logical_or(b != p, q != me))
            def _():
                delta_copy(b, q).wait_send()

        @pl.when(b != p)
        def _():
            base_copy(b).wait_send()
        return carry

    lax.fori_loop(0, pools, drain, 0)


def local(hidden, query_weight_matrix, adapter_down_weight, adapter_up_weight, adapter_index_rows):
    pools = lax.axis_size("pool")
    chips = lax.axis_size("chip")
    shards = lax.axis_size("sub") * chips
    row_count, width = hidden.shape
    cols = query_weight_matrix.shape[1]
    stack, ranks, part = adapter_down_weight.shape
    if 2 + row_count // (pools - 1) > HELD:
        raise ValueError("owner overflow")
    dma = pltpu.SemaphoreType.DMA
    vmem = pl.BlockSpec(memory_space=pltpu.VMEM)
    hbm = pl.BlockSpec(memory_space=pl.ANY)
    return pl.pallas_call(
        functools.partial(kernel, pools, chips, shards, stack),
        out_shape=jax.ShapeDtypeStruct((row_count, width), BF16),
        in_specs=[hbm, hbm, hbm, hbm, hbm],
        out_specs=vmem,
        scratch_shapes=[
            pltpu.VMEM((pools, row_count, width), BF16),
            pltpu.VMEM((pools, 1, META), jnp.int32),
            pltpu.VMEM((row_count, width), BF16),
            pltpu.VMEM((width, cols), BF16),
            pltpu.VMEM((stack * ranks, part), BF16),
            pltpu.VMEM((stack * ranks, part), BF16),
            pltpu.VMEM((pools, SLOTS, row_count), BF16),
            pltpu.VMEM((pools, SLOTS, row_count // 2), BF16),
            pltpu.VMEM((pools, SLOTS, META), BF16),
            pltpu.VMEM((pools, shards, SLOTS, META + part), BF16),
            pltpu.VMEM((pools, shards, SLOTS, META + part), BF16),
            pltpu.VMEM((pools, shards * SLOTS // 2, 128), F32),
            pltpu.VMEM((pools, shards, shards * SLOTS // 2, 128), F32),
            pltpu.VMEM((pools, shards, SLOTS, part - part // 4), BF16),
            pltpu.VMEM((shards, pools * SLOTS, part - part // 4), BF16),
            pltpu.VMEM((pools, row_count, cols), BF16),
            pltpu.VMEM((row_count, width), BF16),
            pltpu.VMEM((row_count, cols), F32),
            pltpu.VMEM((1, row_count), jnp.int32),
            dma((6,)),
            dma((pools, PIECES + 1)),
            dma((pools, PIECES + 1)),
            dma((pools, PIECES + 1)),
            dma((pools, shards)),
            dma((pools, shards)),
            dma((pools, shards)),
            dma((pools, shards)),
            dma((pools,)),
            dma((pools,)),
            dma((pools, shards)),
            dma((pools, shards)),
        ],
        compiler_params=pltpu.CompilerParams(
            collective_id=0, has_side_effects=True, vmem_limit_bytes=48 * 1024 * 1024
        ),
    )(
        *(
            pltpu.with_memory_space_constraint(array, pltpu.HBM)
            for array in (
                hidden,
                adapter_index_rows[None, :],
                query_weight_matrix,
                adapter_down_weight.reshape(stack * ranks, part),
                adapter_up_weight.reshape(stack * ranks, part),
            )
        )
    )


def solution(mesh):
    in_specs = (
        P(("groups", "pool", "sub", "chip"), None),
        P(None, "pool"),
        P("pool", None, ("sub", "chip")),
        P("pool", None, ("sub", "chip")),
        P(("groups", "pool", "sub", "chip")),
    )
    out_specs = P(("groups", "pool", "sub", "chip"), None)
    return jax.shard_map(local, mesh=mesh, in_specs=in_specs, out_specs=out_specs, check_vma=False)
```

```python
import functools

import jax
import jax.numpy as jnp
from jax import lax
from jax.experimental import pallas as pl
from jax.experimental.pallas import tpu as pltpu
from jax.sharding import PartitionSpec as P

ADAPTER_SCALE = 0.5
SLOTS = 16
HELD = 12
META = 128
PIECES = 4
MESH = pl.DeviceIdType.MESH
F32 = jnp.float32
BF16 = jnp.bfloat16


def tile_of(extent):
    return 256 if extent % 256 == 0 else extent


def kernel(
    pools, chips, shards, stack,
    h_hbm, idx_hbm, w_hbm, dn_hbm, up_hbm, out_ref,
    x, xi, own, w, dn, up, chosen, chosen_part, tags, picked, rows, low_out, low, delta, home_delta, base, home_base, acc,
    idx_ref, wsem, hright, hleft, hrecv, rsend, rrecv, lsend, lrecv, bsend, brecv, dsend, drecv,
):
    p = lax.axis_index("pool")
    me = lax.axis_index("sub") * chips + lax.axis_index("chip")
    rows_dev, width = h_hbm.shape
    cols = w.shape[1]
    part = width // shards
    half = width // 2
    quarter = part // 4
    ranks = dn.shape[0] // stack
    tiles = stack * ranks // 256
    each = 256 // ranks
    many = shards * SLOTS

    def where_is(z, sh):
        return {"pool": z, "sub": sh // chips, "chip": sh % chips}

    def rcopy(src, dst, ssem, rsem, z, sh):
        return pltpu.make_async_remote_copy(
            src_ref=src, dst_ref=dst, send_sem=ssem, recv_sem=rsem,
            device_id=where_is(z, sh), device_id_type=MESH,
        )

    peers = [(me + d) % shards for d in range(1, shards)]

    barrier = pltpu.get_barrier_semaphore()

    def greet(z, sh):
        pl.semaphore_signal(barrier, inc=1, device_id=where_is(z, sh), device_id_type=MESH)

    @pl.when(p >= 1)
    def _():
        greet(p - 1, me)

    @pl.when(p + 1 < pools)
    def _():
        greet(p + 1, me)

    for sh in peers:
        greet(p, sh)

    loads = [
        pltpu.make_async_copy(w_hbm.at[pl.ds(0, half)], w.at[pl.ds(0, half)], wsem.at[0]),
        pltpu.make_async_copy(w_hbm.at[pl.ds(half, half)], w.at[pl.ds(half, half)], wsem.at[1]),
        pltpu.make_async_copy(dn_hbm, dn, wsem.at[2]),
        pltpu.make_async_copy(up_hbm, up, wsem.at[3]),
        pltpu.make_async_copy(h_hbm, own, wsem.at[4]),
    ]
    ic = pltpu.make_async_copy(idx_hbm, idx_ref, wsem.at[5])
    ic.start()
    for i in (4, 0, 2, 1, 3):
        loads[i].start()
    ic.wait()

    square = (rows_dev, rows_dev)
    down_axis = lax.broadcasted_iota(jnp.int32, square, 0)
    along = lax.broadcasted_iota(jnp.int32, square, 1)
    index = jnp.broadcast_to(idx_ref[...], square).astype(F32)
    column = jnp.sum(jnp.where(down_axis == along, index, 0.0), axis=1, keepdims=True)
    column = column.astype(jnp.int32)
    owner_column = column // stack
    row_owner = jnp.broadcast_to(idx_ref[...] // stack, square)
    col_owner = jnp.broadcast_to(owner_column, square)
    same = row_owner == col_owner
    ahead = jnp.logical_or(col_owner < row_owner, jnp.logical_and(same, down_axis < along))
    seat_row = jnp.sum(jnp.where(ahead, 1.0, 0.0), axis=0, keepdims=True)
    behind = jnp.logical_or(row_owner < col_owner, jnp.logical_and(same, along < down_axis))
    seat_column = jnp.sum(jnp.where(behind, 1.0, 0.0), axis=1, keepdims=True)
    to_sorted = jnp.where(seat_row == down_axis.astype(F32), 1.0, 0.0).astype(BF16)
    from_sorted = jnp.where(seat_column == along.astype(F32), 1.0, 0.0).astype(BF16)
    lane_index = lax.broadcasted_iota(jnp.int32, (rows_dev, META), 1).astype(F32)
    sorted_index = jnp.where(seat_column == lane_index, column.astype(F32), 0.0)
    xi[p] = jnp.sum(sorted_index, axis=0, keepdims=True).astype(jnp.int32)

    greeters = jnp.minimum(p, 1) + jnp.minimum(pools - 1 - p, 1) + shards - 1
    loads[4].wait()
    for q in range(shards):
        x[p, :, pl.ds(q * part, part)] = jnp.dot(
            to_sorted, own[:, pl.ds(q * part, part)], preferred_element_type=F32
        ).astype(BF16)
    pl.semaphore_wait(barrier, greeters)

    four = pools == 4 and shards == 4
    inner = jnp.logical_and(p >= 1, p + 1 < pools)
    even = p % 2 == 0
    half_rows = rows_dev // 2

    def order(k):
        if four:
            pair = jnp.where(even, p + 1, p - 1)
            second = jnp.where(p < 2, 2, 1)
            third = jnp.where(p < 2, 3, 0)
            return jnp.where(k == 0, p, jnp.where(k == 1, pair, jnp.where(k == 2, second, third)))
        both = jnp.minimum(p, pools - 1 - p)
        near = jnp.where(k % 2 == 1, (k + 1) // 2, -((k + 1) // 2))
        away = jnp.where(p <= pools - 1 - p, k - both, both - k)
        return p + jnp.where(k <= 2 * both, near, away)

    def quarter_of(q):
        return pl.ds(pl.multiple_of(q * part, 128), part)

    def lanes_of(f):
        return pl.ds(f * half, half)

    def to_right(b, i, row, f):
        ref = x.at[b, pl.ds(row, half_rows), lanes_of(f)]
        return rcopy(ref, ref, hright.at[b, i], hrecv.at[b, i], p + 1, me)

    def to_left(b, i, row, f):
        ref = x.at[b, pl.ds(row, half_rows), lanes_of(f)]
        return rcopy(ref, ref, hleft.at[b, i], hrecv.at[b, i], p - 1, me)

    def index_right(b):
        return rcopy(
            xi.at[b], xi.at[b], hright.at[b, PIECES], hrecv.at[b, PIECES], p + 1, me
        )

    def index_left(b):
        return rcopy(
            xi.at[b], xi.at[b], hleft.at[b, PIECES], hrecv.at[b, PIECES], p - 1, me
        )

    def own_right(i):
        return to_right(p, i, half_rows * (1 - i // 2), i % 2)

    def own_left(i):
        return to_left(p, i, half_rows * (i // 2), i % 2)

    @pl.when(p + 1 < pools)
    def _():
        index_right(p).start()

    @pl.when(p >= 1)
    def _():
        index_left(p).start()

    for i in range(PIECES // 2):
        @pl.when(p + 1 < pools)
        def _():
            own_right(i).start()

        @pl.when(p >= 1)
        def _():
            own_left(i).start()

    before = jnp.where(down_axis < along, 1.0, 0.0).astype(BF16)

    def selection(b):
        index = xi[b][:, :rows_dev]
        held_by = index // stack
        local_index = (index - held_by * stack).astype(F32)
        spread_over = (SLOTS, rows_dev)
        owned = jnp.where(jnp.broadcast_to(held_by, spread_over) == p, 1.0, 0.0)
        rank = jnp.dot(owned.astype(BF16), before, preferred_element_type=F32)
        slot = lax.broadcasted_iota(jnp.int32, spread_over, 0).astype(F32)
        taken = jnp.where(rank == slot, owned, 0.0)
        tag = jnp.sum(taken * local_index, axis=1, keepdims=True)
        tags[b] = jnp.broadcast_to(tag, (SLOTS, META)).astype(BF16)
        return taken

    def place_pick(b, q, got):
        got = got.astype(BF16)

        @pl.when(q != me)
        def _():
            picked[b, q, :, pl.ds(0, META)] = tags[b]
            picked[b, q, :, pl.ds(META, part)] = got
            rcopy(picked.at[b, q], rows.at[b, me], rsend.at[b, q], rrecv.at[b, me], p, q).start()

        @pl.when(q == me)
        def _():
            rows[b, me, :, pl.ds(0, META)] = tags[b]
            rows[b, me, :, pl.ds(META, part)] = got

    def pick(b, q):
        place_pick(b, q, jnp.dot(chosen[b], x[b, :, quarter_of(q)], preferred_element_type=F32))

    def pick_part(b, q, at):
        place_pick(
            b, q, jnp.dot(chosen_part[b], x[b, at, quarter_of(q)], preferred_element_type=F32)
        )

    def table(at, values):
        value = values[0]
        for i in range(1, len(values)):
            value = jnp.where(at == i, values[i], value)
        return value

    if four:
        mid_seq = ((1, 0), (2, 0), (1, 1), (2, 1), (2, 2), (1, 2), (2, 3), (1, 3), (3, 0), (3, 1), (3, 2), (3, 3))
        end_seq = ((1, 0), (1, 1), (1, 2), (2, 0), (2, 1), (1, 3), (2, 2), (3, 0), (3, 1), (2, 3), (3, 2), (3, 3))
        arrivals = [
            jnp.where(inner, PIECES * a + b, PIECES * c + d)
            for (a, b), (c, d) in zip(mid_seq, end_seq)
        ]

    def receive(r, carry):
        at = table(r, arrivals) if four else PIECES + r
        k = at // PIECES
        i = at % PIECES
        b = order(k)
        phase = i // 2
        rightward = b < p
        row = pl.multiple_of(half_rows * jnp.where(rightward, 1 - phase, phase), half_rows)
        @pl.when(i == 0)
        def _():
            rcopy(
                xi.at[b], xi.at[b], hright.at[b, PIECES], hrecv.at[b, PIECES], p, peers[0]
            ).wait_recv()

            @pl.when(jnp.logical_and(rightward, p + 1 < pools))
            def _():
                index_right(b).start()

            @pl.when(jnp.logical_and(jnp.logical_not(rightward), p >= 1))
            def _():
                index_left(b).start()

        for f in range(2):
            @pl.when(i % 2 == f)
            def _():
                ref = x.at[b, pl.ds(row, half_rows), lanes_of(f)]
                rcopy(ref, ref, hright.at[b, i], hrecv.at[b, i], p, peers[0]).wait_recv()

                @pl.when(jnp.logical_and(rightward, p + 1 < pools))
                def _():
                    to_right(b, i, row, f).start()

                @pl.when(jnp.logical_and(jnp.logical_not(rightward), p >= 1))
                def _():
                    to_left(b, i, row, f).start()

        first_q = (i % 2) * (shards // 2)

        @pl.when(jnp.logical_and(inner, phase == 1))
        def _():
            @pl.when(i % 2 == 0)
            def _():
                chosen[b] = selection(b).astype(BF16)

            def one(q, c):
                pick(b, first_q + q)
                return c

            lax.fori_loop(0, shards // 2, one, 0)

        @pl.when(jnp.logical_and(jnp.logical_not(inner), phase == 0))
        def _():
            part_rows = pl.ds(row, half_rows)

            @pl.when(i % 2 == 0)
            def _():
                taken = selection(b)
                kept = jnp.where(row > 0, taken[:, half_rows:], taken[:, :half_rows])
                chosen_part[b] = kept.astype(BF16)

            def one(q, c):
                pick_part(b, first_q + q, part_rows)
                return c

            lax.fori_loop(0, shards // 2, one, 0)
        return carry

    def project(b, k, last):
        tile = tile_of(cols)

        for j in range(cols // tile):
            at = pl.ds(j * tile, tile)
            term = jnp.dot(
                x[b, :, pl.ds(k * half, half)], w[pl.ds(k * half, half), at],
                preferred_element_type=F32,
            )
            if last:
                base[b, :, at] = (acc[:, at] + term).astype(BF16)
            else:
                acc[:, at] = term

    mine_cols = pl.ds(pl.multiple_of(p * cols, 128), cols)
    mine_slots = pl.ds(pl.multiple_of(p * SLOTS, SLOTS), SLOTS)

    def base_copy(b):
        return rcopy(base.at[b], home_base.at[:, mine_cols], bsend.at[b], brecv.at[p], b, me)

    def delta_copy(b, sh):
        return rcopy(
            delta.at[b, sh], home_delta.at[me, mine_slots], dsend.at[b, sh], drecv.at[p, me], b, sh
        )

    lane = lax.broadcasted_iota(jnp.int32, (many, 256), 1) // ranks
    lower = lax.broadcasted_iota(jnp.int32, (many // 2, 128), 1) < 64

    def adapter_of(b):
        tag = rows[b, :, :, pl.ds(0, META)].reshape(many, META).astype(F32)
        return tag[:, 1:2].astype(jnp.int32)

    def shrink(b):
        for sh in peers:
            rcopy(rows.at[b, sh], rows.at[b, sh], rsend.at[b, sh], rrecv.at[b, sh], p, sh).wait_recv()
        adapter = adapter_of(b)
        here = rows[b, :, :, pl.ds(META, part)].reshape(many, part)
        total = jnp.zeros((many, 128), F32)
        for j in range(tiles):
            term = lax.dot_general(
                here, dn[pl.ds(j * 256, 256), :], (((1,), (1,)), ((), ())),
                preferred_element_type=F32,
            )
            term = jnp.where(lane + j * each == adapter, term, 0.0)
            total = total + term[:, :128] + term[:, 128:]
        total = total + pltpu.roll(total, 64, 1)
        packed = jnp.where(lower, total[: many // 2], total[many // 2 :])
        low_out[b] = packed
        low[b, me] = packed
        for sh in peers:
            rcopy(low_out.at[b], low.at[b, me], lsend.at[b, sh], lrecv.at[b, me], p, sh).start()

    def grow(b):
        for sh in peers:
            rcopy(low_out.at[b], low.at[b, sh], lsend.at[b, sh], lrecv.at[b, sh], p, sh).wait_recv()
        adapter = adapter_of(b)
        both = low[b, 0]
        for sh in range(1, shards):
            both = both + low[b, sh]
        both = both.astype(BF16).astype(F32)
        turned = pltpu.roll(both, 64, 1)
        full = jnp.concatenate(
            [jnp.where(lower, both, turned), jnp.where(lower, turned, both)], axis=0
        )
        full = jnp.concatenate([full, full], axis=1)
        spread = jnp.concatenate(
            [
                jnp.where(lane + j * each == adapter, full, 0.0).astype(BF16)
                for j in range(tiles)
            ],
            axis=1,
        )
        rest = jnp.dot(spread, up[:, pl.ds(3 * quarter, quarter)], preferred_element_type=F32)
        top = lax.broadcasted_iota(jnp.int32, (many, quarter), 0) % SLOTS < HELD
        for j in range(3):
            at = pl.ds(j * quarter, quarter)
            term = jnp.dot(spread, up[:, at], preferred_element_type=F32)
            term = jnp.where(top, term, pltpu.roll(rest, HELD - 4 * j, 0))
            delta[b, :, :, at] = (ADAPTER_SCALE * term).astype(BF16).reshape(shards, SLOTS, quarter)

    def give(b):
        for sh in range(shards):
            @pl.when(jnp.logical_or(b != p, sh != me))
            def _():
                delta_copy(b, sh).start()

            @pl.when(jnp.logical_and(b == p, sh == me))
            def _():
                home_delta[me, mine_slots] = delta[b, sh]

    def give_base(b):
        @pl.when(b != p)
        def _():
            base_copy(b).start()

        @pl.when(b == p)
        def _():
            home_base[:, mine_cols] = base[b]

    chosen[p] = selection(p).astype(BF16)

    def own_pick(q, c):
        pick(p, q)
        return c

    lax.fori_loop(0, shards, own_pick, 0)

    for i in range(PIECES // 2, PIECES):
        @pl.when(p + 1 < pools)
        def _():
            own_right(i).start()

        @pl.when(p >= 1)
        def _():
            own_left(i).start()


    PA, S, PB, G = range(4)
    if four:
        mid_plan = ((0, PA, 0), (0, S, 0), (0, PB, 4), (2, PA, 8), (2, PB, 8), (2, S, 9), (3, PA, 11), (0, G, 12), (2, G, 12), (3, PB, 12), (3, S, 12), (1, S, 12), (1, PA, 12), (1, PB, 12), (3, G, 12), (1, G, 12))
        end_plan = ((0, PA, 0), (0, S, 0), (0, PB, 0), (0, G, 2), (1, S, 4), (1, PA, 4), (1, PB, 6), (2, S, 6), (1, G, 7), (2, G, 9), (2, PA, 10), (2, PB, 12), (3, S, 12), (3, PA, 12), (3, PB, 12), (3, G, 12))
        plan = [
            jnp.where(inner, 256 * d + 16 * a + b, 256 * g + 16 * e + f)
            for (a, b, d), (e, f, g) in zip(mid_plan, end_plan)
        ]

    def chunk(c, done):
        if four:
            at = table(c, plan)
            ready = at // 256
            k = (at // 16) % 16
            j = at % 16
        else:
            ready = PIECES * (c // 4)
            k = c // 4
            j = c % 4
        lax.fori_loop(done, ready, receive, 0)
        b = order(k)

        @pl.when(j == PA)
        def _():
            @pl.when(k == 0)
            def _():
                loads[0].wait()
            project(b, 0, False)

        @pl.when(j == S)
        def _():
            @pl.when(k == 0)
            def _():
                loads[2].wait()
            shrink(b)

        @pl.when(j == PB)
        def _():
            @pl.when(k == 0)
            def _():
                loads[1].wait()
            project(b, 1, True)
            give_base(b)

        @pl.when(j == G)
        def _():
            @pl.when(k == 0)
            def _():
                loads[3].wait()
            grow(b)
            give(b)
        return ready

    lax.fori_loop(0, 4 * pools, chunk, 0)

    slots = pools * SLOTS
    lanes = lax.broadcasted_iota(jnp.int32, (rows_dev, slots), 1)
    owner = jnp.where(owner_column == lanes // SLOTS, 1.0, 0.0)
    after = jnp.where(down_axis > along, 1.0, 0.0).astype(BF16)
    rank = jnp.dot(after, owner.astype(BF16), preferred_element_type=F32)
    seat = lanes % SLOTS
    place = jnp.where(rank == seat.astype(F32), owner, 0.0).astype(BF16)
    tails = [
        jnp.where(
            jnp.logical_and(seat >= HELD, rank == (seat - HELD + 4 * k).astype(F32)), owner, 0.0
        ).astype(BF16)
        for k in range(3)
    ]

    places = jnp.concatenate([place] + tails, axis=0)

    def base_wait(z, carry):
        @pl.when(z != p)
        def _():
            dst = home_base.at[:, pl.ds(pl.multiple_of(z * cols, 128), cols)]
            rcopy(base.at[z], dst, bsend.at[z], brecv.at[z], z, me).wait_recv()
        return carry

    lax.fori_loop(0, pools, base_wait, 0)

    def mine(at):
        return jnp.dot(from_sorted, home_base[:, at], preferred_element_type=F32)

    for sh in range(shards):
        def delta_wait(z, carry):
            @pl.when(jnp.logical_or(z != p, sh != me))
            def _():
                dst = home_delta.at[sh, pl.ds(pl.multiple_of(z * SLOTS, SLOTS), SLOTS)]
                rcopy(delta.at[z, sh], dst, dsend.at[z, sh], drecv.at[z, sh], z, sh).wait_recv()
            return carry

        lax.fori_loop(0, pools, delta_wait, 0)
        start = sh * part
        wide = 3 * quarter
        term = jnp.dot(places, home_delta[sh], preferred_element_type=F32)
        at = pl.ds(start, wide)
        out_ref[:, at] = (mine(at) + term[:rows_dev]).astype(BF16)
        rest = term[rows_dev : 2 * rows_dev, :quarter]
        rest = rest + term[2 * rows_dev : 3 * rows_dev, quarter : 2 * quarter]
        rest = rest + term[3 * rows_dev :, 2 * quarter :]
        at = pl.ds(start + wide, quarter)
        out_ref[:, at] = (mine(at) + rest).astype(BF16)

    def drain(b, carry):
        @pl.when(jnp.logical_and(b <= p, p + 1 < pools))
        def _():
            index_right(b).wait_send()

        @pl.when(jnp.logical_and(b >= p, p >= 1))
        def _():
            index_left(b).wait_send()

        for i in range(PIECES):
            @pl.when(jnp.logical_and(b <= p, p + 1 < pools))
            def _():
                to_right(b, i, half_rows * (1 - i // 2), i % 2).wait_send()

            @pl.when(jnp.logical_and(b >= p, p >= 1))
            def _():
                to_left(b, i, half_rows * (i // 2), i % 2).wait_send()

        for q in range(shards):
            @pl.when(q != me)
            def _():
                rcopy(picked.at[b, q], rows.at[b, me], rsend.at[b, q], rrecv.at[b, me], p, q).wait_send()
                rcopy(low_out.at[b], low.at[b, me], lsend.at[b, q], lrecv.at[b, me], p, q).wait_send()

            @pl.when(jnp.logical_or(b != p, q != me))
            def _():
                delta_copy(b, q).wait_send()

        @pl.when(b != p)
        def _():
            base_copy(b).wait_send()
        return carry

    lax.fori_loop(0, pools, drain, 0)


def local(hidden, query_weight_matrix, adapter_down_weight, adapter_up_weight, adapter_index_rows):
    pools = lax.axis_size("pool")
    chips = lax.axis_size("chip")
    shards = lax.axis_size("sub") * chips
    row_count, width = hidden.shape
    cols = query_weight_matrix.shape[1]
    stack, ranks, part = adapter_down_weight.shape
    if 2 + row_count // (pools - 1) > HELD:
        raise ValueError("owner overflow")
    dma = pltpu.SemaphoreType.DMA
    vmem = pl.BlockSpec(memory_space=pltpu.VMEM)
    hbm = pl.BlockSpec(memory_space=pl.ANY)
    return pl.pallas_call(
        functools.partial(kernel, pools, chips, shards, stack),
        out_shape=jax.ShapeDtypeStruct((row_count, width), BF16),
        in_specs=[hbm, hbm, hbm, hbm, hbm],
        out_specs=vmem,
        scratch_shapes=[
            pltpu.VMEM((pools, row_count, width), BF16),
            pltpu.VMEM((pools, 1, META), jnp.int32),
            pltpu.VMEM((row_count, width), BF16),
            pltpu.VMEM((width, cols), BF16),
            pltpu.VMEM((stack * ranks, part), BF16),
            pltpu.VMEM((stack * ranks, part), BF16),
            pltpu.VMEM((pools, SLOTS, row_count), BF16),
            pltpu.VMEM((pools, SLOTS, row_count // 2), BF16),
            pltpu.VMEM((pools, SLOTS, META), BF16),
            pltpu.VMEM((pools, shards, SLOTS, META + part), BF16),
            pltpu.VMEM((pools, shards, SLOTS, META + part), BF16),
            pltpu.VMEM((pools, shards * SLOTS // 2, 128), F32),
            pltpu.VMEM((pools, shards, shards * SLOTS // 2, 128), F32),
            pltpu.VMEM((pools, shards, SLOTS, part - part // 4), BF16),
            pltpu.VMEM((shards, pools * SLOTS, part - part // 4), BF16),
            pltpu.VMEM((pools, row_count, cols), BF16),
            pltpu.VMEM((row_count, width), BF16),
            pltpu.VMEM((row_count, cols), F32),
            pltpu.VMEM((1, row_count), jnp.int32),
            dma((6,)),
            dma((pools, PIECES + 1)),
            dma((pools, PIECES + 1)),
            dma((pools, PIECES + 1)),
            dma((pools, shards)),
            dma((pools, shards)),
            dma((pools, shards)),
            dma((pools, shards)),
            dma((pools,)),
            dma((pools,)),
            dma((pools, shards)),
            dma((pools, shards)),
        ],
        compiler_params=pltpu.CompilerParams(
            collective_id=0, has_side_effects=True, vmem_limit_bytes=48 * 1024 * 1024
        ),
    )(
        *(
            pltpu.with_memory_space_constraint(array, pltpu.HBM)
            for array in (
                hidden,
                adapter_index_rows[None, :],
                query_weight_matrix,
                adapter_down_weight.reshape(stack * ranks, part),
                adapter_up_weight.reshape(stack * ranks, part),
            )
        )
    )


def solution(mesh):
    in_specs = (
        P(("groups", "pool", "sub", "chip"), None),
        P(None, "pool"),
        P("pool", None, ("sub", "chip")),
        P("pool", None, ("sub", "chip")),
        P(("groups", "pool", "sub", "chip")),
    )
    out_specs = P(("groups", "pool", "sub", "chip"), None)
    return jax.shard_map(local, mesh=mesh, in_specs=in_specs, out_specs=out_specs, check_vma=False)
```
